128 devices in a mesh: rep: 16 (over y, x_lo, core), blk: 8 (over z, x_hi).
Axes of the slice: x: 4 (x_hi: 2, x_lo: 2; x = x_hi * 2 + x_lo), y: 4, z: 4, core: 2. Of those that a mesh axis runs over, the one named last changes fastest.
Arguments:
- tokens: bfloat16 [16384, 1536], P(('rep', 'blk')), may hold values from -64 to 64
- attn_in: float32 [1536, 2048], P(('rep', 'blk')), may hold values from -8 to 8
- attn_out: float32 [1536, 1536], P(('rep', 'blk')), may hold values from -0.15625 to 0.15625
- expert_in: float32 [16, 1536, 1536], P(None, ('rep', 'blk')), may hold values from -0.15625 to 0.15625
- expert_out: float32 [16, 768, 1536], P(None, ('rep', 'blk')), may hold values from -0.21875 to 0.21875
- attn_gain: float32 [1536], replicated, may hold values from 0.25 to 1.75
- moe_gain: float32 [1536], replicated, may hold values from 0.25 to 1.75
- lengths: int32 [16, 6], P('rep'), may hold values from 1 to 512, 1024 in all within a row
- page_table: int32 [16, 8], P('rep'), may hold values from 0 to 7, each once within a row
- routes: int32 [16384, 4], P(('rep', 'blk')), may hold values from 0 to 15, all different within a row; in each aligned block of 128 rows (0 to 127, 128 to 255, ...) at most 64 rows name the same one
- gates: bfloat16 [16384, 4], P(('rep', 'blk')), may hold values from 0.19921875 to 1
Outputs:
- mixed: bfloat16 [16384, 1536], P(('rep', 'blk'))
- kv_cache: bfloat16 [128, 128, 512], P(('rep', 'blk'))
The draws below stay inside these ranges and needn't reach their ends.
Inputs may be any that keep to these rules, and one draw needn't show every extreme that they name: Each replica's lengths sum to 1024. `page_table`: each replica's row is a permutation of its 8 pages. `routes`: a token names 4 different experts; among the rows of one device no expert is named more than 64 times.
All inputs are finite; a program needn't handle non-finite values.
Results may differ from the reference program's by a relative error of at most 0.013.
Values may be sent and summed in bfloat16 or wider, within the bound.
A program may use at most 128 MiB of HBM per device.

```python
import math
import jax
import jax.numpy as jnp
import numpy as np
from jax import lax

D = 1536
FF = 768
QH = 12
KVH = 2
HD = 128
TOP = 4
E = 16
PAGE = 128
SEQS = 6
TOK_DEV = 128
GROUP = 1024
TOKENS = 16384
PAGES = 8
MAXLEN = 512
CAP = 64
QW = 1536
KVW = 512
QKV = 2048
N_REP = 16
N_BLK = 8


def draw_tokens(key, part):
    first = jax.random.fold_in(key, 0)
    values = jax.random.truncated_normal(first, -6.0, 6.0, (TOKENS, D), jnp.float32)
    return values.astype(jnp.bfloat16)


def draw_attn_in(key, part):
    first = jax.random.fold_in(key, 0)
    base = jax.random.truncated_normal(first, -6.0, 6.0, (D, QKV), jnp.float32) / jnp.sqrt(jnp.float32(D))
    return jnp.clip(base, -8.0, 8.0)


def level_of(own_key, shape, cuts, smallest, high):
    loudness, own = 1.0, jax.random.fold_in(own_key, 6)
    for dim, shards_of in cuts:
        draws = jnp.exp(jax.random.uniform(jax.random.fold_in(own, dim), (shards_of,), jnp.float32, smallest / len(cuts), high / len(cuts)))
        loudness = loudness * jnp.repeat(draws, shape[dim] // shards_of).reshape([-1 if axis == dim else 1 for axis in range(len(shape))])
    return loudness


def length_profile(count, total, limit, slope):
    loads = [(1 << 20) // math.isqrt(grade ** slope) + 1 for grade in range(2, count + 1)]
    rest, counts = total - limit - (count - 1), [1] * (count - 1)
    while rest > 0:
        free = [i for i in range(count - 1) if counts[i] < limit]
        mass, left = sum([loads[i] for i in free]), rest
        for i in free:
            addition = min(limit - counts[i], max(1, left * loads[i] // mass), rest)
            counts[i] = counts[i] + addition
            rest = rest - addition
    return np.array([limit] + counts)


def ragged_sizes(own_key, number_of, total, reach, skew):
    if number_of == 2:
        one = jax.random.randint(own_key, (), max(1, total - reach), min(reach, total - 1) + 1)
        return jnp.stack([one, total - one])
    sizes = jnp.asarray(length_profile(number_of, total, reach, skew), jnp.int32)
    twos = (number_of - 1) // 2
    donor, taker = sizes[1:1 + 2 * twos:2], sizes[2:2 + 2 * twos:2]
    slack = jnp.minimum(donor - 1, reach - taker)
    moved = jax.random.randint(jax.random.fold_in(own_key, 1), (twos,), 0, 1 << 20) % (slack + 1)
    sizes = sizes.at[1:1 + 2 * twos:2].set(donor - moved).at[2:2 + 2 * twos:2].set(taker + moved)
    return sizes[jax.random.permutation(jax.random.fold_in(own_key, 2), number_of)]


def routed_block(stream_key, own, number, rows, amount, top, limit, slope):
    order = jax.random.permutation(stream_key, amount)
    crowded, ordinary = shares(amount, rows * top, limit, slope, True), shares(amount, rows * top, limit, slope, False)
    places = jnp.arange(amount)

    def named(tallies, rotation):
        used = int((tallies > 0).sum())
        fixed = max(1, used // 4)
        shifted = fixed + (places - fixed + rotation * (used - fixed)) % max(1, amount - fixed)
        return jnp.zeros((amount,), jnp.int32).at[order[jnp.where(places < fixed, places, shifted)]].set(jnp.asarray(tallies, jnp.int32))

    tallies = jnp.where(number % 4 == 0, named(crowded, number // 4), named(ordinary, number - number // 4 - 1))
    mixed = jax.random.permutation(jax.random.fold_in(own, 3), amount)
    donor, receiver = mixed[0:amount // 2 * 2:2], mixed[1:amount // 2 * 2:2]
    margin = jnp.minimum(tallies[donor] - 1, limit - tallies[receiver]) // 2
    margin = jnp.where((donor == order[0]) | (receiver == order[0]) | (tallies[receiver] == 0), 0, jnp.maximum(margin, 0))
    shifted = jax.random.randint(jax.random.fold_in(own, 4), (amount // 2,), 0, 1 << 20) % (margin + 1)
    tallies = tallies.at[donor].add(-shifted).at[receiver].add(shifted)
    members = jnp.searchsorted(jnp.cumsum(tallies), jnp.arange(rows * top), side="right").astype(jnp.int32)
    grid = members.reshape(top, rows).T
    grid = grid[jax.random.permutation(jax.random.fold_in(own, 1), rows)]
    rotation = jax.random.randint(jax.random.fold_in(own, 2), (rows, 1), 0, top)
    return jnp.take_along_axis(grid, (jnp.arange(top)[None, :] + rotation) % top, axis=1)


def shares(amount, total, bound, skew, full):
    weights = [(1 << 20) // math.isqrt(rank ** skew) + 1 for rank in range(1, amount + 1)]
    largest = bound if full else min(bound, max(-(-total // amount), total * weights[0] // sum(weights)))
    least = 1 if total - largest >= amount - 1 else 0
    holding, rest = [largest] + [least] * (amount - 1), total - largest - least * (amount - 1)
    while rest > 0:
        candidates = [i for i in range(1, amount) if holding[i] < largest] or [i for i in range(1, amount) if holding[i] < bound]
        pool, left = sum([weights[i] for i in candidates]), rest
        for i in candidates:
            more = min(bound - holding[i], max(1, left * weights[i] // pool), rest)
            holding[i] = holding[i] + more
            rest = rest - more
    return np.array(holding)


def gaussian(own_key, dims, width, limit, pieces=(), kind=jnp.bfloat16):
    values = jax.random.normal(own_key, dims, jnp.float32) * width
    if len(pieces) > 0:
        values = level_of(own_key, dims, pieces, -0.22, 0.18) * values
    return jnp.clip(values, min=-limit, max=limit).astype(kind)


def setup_inputs(seed: int = 0) -> dict:
    splits = jax.random.split(jax.random.key(seed), 12)
    tokens = draw_tokens(jax.random.fold_in(splits[11], 71), 0)
    attn_in = draw_attn_in(jax.random.fold_in(splits[11], 71), 0)
    attn_out = gaussian(splits[2], (QW, D), QW ** -0.5, 0.15625, ((0, 128),), jnp.float32)
    expert_in = gaussian(splits[3], (E, D, 2 * FF), D ** -0.5, 0.15625, ((1, 128),), jnp.float32)
    expert_out = gaussian(splits[4], (E, FF, D), FF ** -0.5, 0.21875, ((1, 128),), jnp.float32)
    attn_gain = jnp.clip(1.0 + 0.15 * jax.random.normal(splits[5], (D,), jnp.float32), 0.25, 1.75)
    moe_gain = jnp.clip(1.0 + 0.15 * jax.random.normal(splits[6], (D,), jnp.float32), 0.25, 1.75)
    lengths = jax.vmap(lambda own: ragged_sizes(own, SEQS, GROUP, MAXLEN, 2))(jax.random.split(splits[7], N_REP)).reshape((N_REP, SEQS)).astype(jnp.int32)
    page_table = jax.vmap(lambda own: jax.random.permutation(own, PAGES))(jax.random.split(splits[8], N_REP)).reshape((N_REP, PAGES)).astype(jnp.int32)
    routes_keys = jax.random.split(jax.random.fold_in(splits[9], 1), TOKENS // TOK_DEV)
    routes_turns = jax.random.permutation(jax.random.fold_in(splits[9], 3), TOKENS // TOK_DEV)
    routes = jax.vmap(lambda own, number: routed_block(jax.random.fold_in(splits[9], 2), own, number, TOK_DEV, E, TOP, CAP, 2))(routes_keys, routes_turns).reshape((TOKENS, TOP))
    gates = jnp.clip(jnp.exp(math.log(1.0) - 1.6133518 * jax.random.uniform(splits[10], (TOKENS, TOP), jnp.float32) ** level_of(splits[10], (TOKENS, TOP), ((0, 128),), -0.2, 0.2)), 0.19921875, 1.0).astype(jnp.bfloat16)
    return {"tokens": tokens, "attn_in": attn_in, "attn_out": attn_out, "expert_in": expert_in, "expert_out": expert_out, "attn_gain": attn_gain, "moe_gain": moe_gain, "lengths": lengths, "page_table": page_table, "routes": routes, "gates": gates}


def rms_scale(values, gain):
    values = values.astype(jnp.float32)
    mean_sq = lax.optimization_barrier(jnp.mean(values * values, axis=-1, keepdims=True))
    return values * lax.rsqrt(mean_sq + 1e-06) * gain

def rotate(values, position):
    half = values.shape[-1] // 2
    steps_all = jnp.arange(half, dtype=jnp.float32)
    frequency = jnp.exp(steps_all * (-2.0 * math.log(10000.0) / values.shape[-1]))
    angle = position[:, None] * frequency[None, :]
    cosine = jnp.cos(angle)[:, None, :]
    sine = jnp.sin(angle)[:, None, :]
    front = values[..., :half]
    behind = values[..., half:]
    return jnp.concatenate([front * cosine - behind * sine, behind * cosine + front * sine], axis=-1)

def segment_info(lengths, count):
    lengths = lengths.astype(jnp.int32)
    starts = (jnp.cumsum(lengths) - lengths).astype(jnp.int32)
    index = jnp.arange(count, dtype=jnp.int32)
    member = (index[:, None] >= starts[None, :]).astype(jnp.int32)
    segment = (lax.optimization_barrier(jnp.sum(member, axis=1)) - 1).astype(jnp.int32)
    owner = segment[:, None] == jnp.arange(lengths.shape[0], dtype=jnp.int32)[None, :]
    begin = lax.optimization_barrier(jnp.sum(jnp.where(owner, starts[None, :], 0), axis=1)).astype(jnp.int32)
    return (segment, (index - begin).astype(jnp.int32))

def one_group(tokens, lengths, table, routes, gates, w_qkv, w_mix, w_in, w_out, attn_gain, moe_gain):
    count = tokens.shape[0]
    heads_per = QH // KVH
    segment, position = segment_info(lengths, count)
    index = jnp.arange(count, dtype=jnp.int32)
    normed = rms_scale(tokens, attn_gain).astype(jnp.bfloat16)
    projected = jnp.dot(normed, w_qkv, preferred_element_type=jnp.float32)
    angle_pos = position.astype(jnp.float32)
    queries = rotate(projected[:, :QW].reshape(count, QH, HD), angle_pos).astype(jnp.bfloat16)
    keys = rotate(projected[:, QW:QW + KVH * HD].reshape(count, KVH, HD), angle_pos).astype(jnp.bfloat16)
    values = projected[:, QW + KVH * HD:].astype(jnp.bfloat16)
    grouped = queries.reshape(count, KVH, heads_per, HD).astype(jnp.float32)
    scores = jnp.einsum('igrd,jgd->grij', grouped, keys.astype(jnp.float32)) / math.sqrt(HD)
    allowed = (segment[:, None] == segment[None, :]) & (index[None, :] <= index[:, None])
    scores = jnp.where(allowed[None, None], scores, jnp.float32(-1e+30))
    highest = lax.optimization_barrier(jnp.max(scores, axis=-1, keepdims=True))
    weights = jnp.exp(scores - highest)
    probs = (weights / lax.optimization_barrier(jnp.sum(weights, axis=-1, keepdims=True))).astype(jnp.bfloat16)
    value_heads = values.reshape(count, KVH, HD).astype(jnp.float32)
    attended = jnp.einsum('grij,jgd->igrd', probs.astype(jnp.float32), value_heads)
    attended = attended.astype(jnp.bfloat16).reshape(count, QW)
    hidden = tokens.astype(jnp.float32) + jnp.dot(attended, w_mix, preferred_element_type=jnp.float32)
    normed_two = rms_scale(hidden, moe_gain).astype(jnp.bfloat16)
    depth = N_BLK * CAP

    def add_expert(total, expert):
        hits = routes == expert
        routed = jnp.any(hits, axis=1)
        weight = lax.optimization_barrier(jnp.sum(jnp.where(hits, gates.astype(jnp.float32), jnp.float32(0.0)), axis=1))
        order = jnp.argsort(jnp.where(routed, index, index + count))[:depth].astype(jnp.int32)
        chosen = normed_two[order]
        gate_up = jnp.dot(chosen, w_in[expert], preferred_element_type=jnp.float32)
        activated = (jax.nn.relu(gate_up[:, :FF]) * gate_up[:, FF:]).astype(jnp.bfloat16)
        result = jnp.dot(activated, w_out[expert], preferred_element_type=jnp.float32).astype(jnp.bfloat16)
        return (total.at[order].add(weight[order][:, None] * result.astype(jnp.float32)), None)
    expert_term, _ = lax.scan(add_expert, jnp.zeros((count, D), jnp.float32), jnp.arange(E, dtype=jnp.int32))
    mixed = (hidden + expert_term).astype(jnp.bfloat16)
    cache = jnp.concatenate([keys.reshape(count, KVH * HD), values], axis=1).reshape(count // PAGE, PAGE, KVW)
    pages = jnp.zeros_like(cache).at[table.astype(jnp.int32)].set(cache)
    return (mixed, pages)

def reference(tokens, attn_in, attn_out, expert_in, expert_out, attn_gain, moe_gain, lengths, page_table, routes, gates):
    w_qkv = attn_in.astype(jnp.bfloat16)
    w_mix = attn_out.astype(jnp.bfloat16)
    w_in = expert_in.astype(jnp.bfloat16)
    w_out = expert_out.astype(jnp.bfloat16)

    def run(item):
        group_tokens, group_lengths, group_table, group_routes, group_gates = item
        return one_group(group_tokens, group_lengths, group_table, group_routes, group_gates, w_qkv, w_mix, w_in, w_out, attn_gain, moe_gain)
    mixed, pages = lax.map(run, (tokens.reshape(N_REP, GROUP, D), lengths, page_table, routes.reshape(N_REP, GROUP, TOP), gates.reshape(N_REP, GROUP, TOP)))
    return (mixed.reshape(TOKENS, D), pages.reshape(N_REP * PAGES, PAGE, KVW))
```

```python
import functools
import math

import jax
import jax.numpy as jnp
from jax import lax
from jax.experimental import pallas as pl
from jax.experimental.pallas import tpu as pltpu
from jax.sharding import PartitionSpec as P

D = 1536
FF = 768
QH = 12
KVH = 2
HD = 128
E = 16
PAGE = 128
CAP = 64
QW = 1536
BF = jnp.bfloat16
F32 = jnp.float32
MESH = pl.DeviceIdType.MESH


def rms_scale(values, gain):
    values = values.astype(jnp.float32)
    mean_sq = jnp.mean(values * values, axis=-1, keepdims=True)
    return values * lax.rsqrt(mean_sq + 1e-06) * gain


def rotate(values, position):
    half = values.shape[-1] // 2
    steps_all = jnp.arange(half, dtype=jnp.float32)
    frequency = jnp.exp(steps_all * (-2.0 * math.log(10000.0) / values.shape[-1]))
    angle = position[:, None] * frequency[None, :]
    cosine = jnp.cos(angle)[:, None, :]
    sine = jnp.sin(angle)[:, None, :]
    front = values[..., :half]
    behind = values[..., half:]
    return jnp.concatenate(
        [front * cosine - behind * sine, behind * cosine + front * sine], axis=-1
    )


def segment_info(lengths, count):
    starts = jnp.cumsum(lengths) - lengths
    index = jnp.arange(count, dtype=jnp.int32)
    member = (index[:, None] >= starts[None, :]).astype(jnp.int32)
    segment = jnp.sum(member, axis=1) - 1
    owner = segment[:, None] == jnp.arange(lengths.shape[0], dtype=jnp.int32)[None, :]
    begin = jnp.sum(jnp.where(owner, starts[None, :], 0), axis=1)
    return (segment, index - begin)


def slot_tables(weight, depth):
    member = (weight > 0).astype(jnp.int32)
    ranked = jnp.cumsum(member, axis=0) - 1
    slot_ids = jnp.arange(depth, dtype=jnp.int32)
    hit = (member.T[:, None, :] == 1) & (ranked.T[:, None, :] == slot_ids[None, :, None])
    onehot = hit.astype(jnp.bfloat16)
    gated = jnp.where(hit, weight.T[:, None, :], jnp.zeros((), jnp.bfloat16))
    return (onehot, gated)


class Net:
    def __init__(self, send_sems, recv_sems):
        rep, blk = lax.axis_index("rep"), lax.axis_index("blk")
        self.y, self.xl, self.c = rep // 4, (rep // 2) % 2, rep % 2
        self.z, self.xh = blk // 2, blk % 2
        self.x = self.xh * 2 + self.xl
        self.ss, self.rs, self.used = send_sems, recv_sems, 0

    def dev(self, y=0, x=0, z=0, c=0):
        yy = (self.y + y) % 4
        xx = (self.x + x) % 4
        zz = (self.z + z) % 4
        cc = (self.c + c) % 2
        return ((yy * 2 + xx % 2) * 2 + cc, zz * 2 + xx // 2)

    def xflip(self):
        return (((self.y * 2 + 1 - self.xl) * 2) + self.c, self.z * 2 + self.xh)

    def take(self, n=1):
        k = self.used
        self.used = k + n
        return k

    def make(self, src, dst, to, k):
        return pltpu.make_async_remote_copy(
            src_ref=src,
            dst_ref=dst,
            send_sem=self.ss.at[k],
            recv_sem=self.rs.at[k],
            device_id=to,
            device_id_type=MESH,
        )

    def send(self, ref, to):
        cp = self.make(ref, ref, to, self.take())
        cp.start()
        return cp


def enter(net):
    barrier = pltpu.get_barrier_semaphore()
    around = [net.dev(x=1), net.dev(x=3), net.dev(c=1)]
    around += [net.dev(y=k) for k in (1, 2, 3)]
    around += [net.dev(z=dz, x=dx) for dz in range(4) for dx in (0, 2) if dz or dx]
    for to in around:
        pl.semaphore_signal(barrier, inc=1, device_id=to, device_id_type=MESH)
    pl.semaphore_wait(barrier, len(around))


def gather_weights(net, qs, ms, es, os, q1, m1, e1, o1, wq, wm, wi, wo):
    y, xl, c, z, xh = net.y, net.xl, net.c, net.z, net.xh
    sent = []
    half = z // 2
    slot = (z % 2) * 2 + xh
    first = {}
    for name, src, dst in (("q", qs, q1), ("m", ms, m1)):
        base_s, base_r = net.take(4), net.used - 4
        for k in range(4):
            zt = (z + k) % 4
            cp = pltpu.make_async_remote_copy(
                src_ref=src.at[zt],
                dst_ref=dst.at[slot],
                send_sem=net.ss.at[base_s + k],
                recv_sem=net.rs.at[base_r + slot],
                device_id=((y * 2 + xl) * 2 + c, zt * 2 + half),
                device_id_type=MESH,
            )
            if k == 0:

                @pl.when(half != xh)
                def _(cp=cp):
                    cp.start()

                @pl.when(half == xh)
                def _(src=src, dst=dst):
                    dst[pl.ds(slot, 1)] = src[pl.ds(z, 1)]

            else:
                cp.start()
            first[name, k] = cp
    blk = z * 2 + xh
    for name, src, dst in (("e", es, e1), ("o", os, o1)):
        base = net.take(8)
        for k in range(1, 8):
            to = (blk + k) % 8
            cp = pltpu.make_async_remote_copy(
                src_ref=src.at[pl.ds(2 * to, 2)],
                dst_ref=dst.at[blk],
                send_sem=net.ss.at[base + k],
                recv_sem=net.rs.at[base + k],
                device_id=((y * 2 + xl) * 2 + c, to),
                device_id_type=MESH,
            )
            cp.start()
            first[name, k] = cp
        dst[pl.ds(blk, 1)] = src[pl.ds(2 * blk, 2)][None]

    def wait_first(name, src, dst, base):
        for j in range(4):
            mine = (z == 2 * xh + j // 2) & (xh == j % 2)

            @pl.when(jnp.logical_not(mine))
            def _(j=j):
                net.make(src.at[0], dst.at[0], net.dev(c=1), base + j).wait_recv()

    def stack(pieces):
        return jnp.concatenate([p.astype(F32) for p in pieces], axis=0).astype(BF)

    wait_first("q", qs, q1, 0)
    block = stack([q1[j] for j in range(4)])
    ca = pl.ds(pl.multiple_of(z * 256, 256), 256)
    cb = pl.ds(pl.multiple_of(1024 + z * 256, 256), 256)
    cm = pl.ds(pl.multiple_of(z * 384, 128), 384)
    wq[y, xl, c, xh, :, ca] = block[:, :256]
    wq[y, xl, c, xh, :, cb] = block[:, 256:]
    wait_first("m", ms, m1, 4)
    wm[y, xl, c, xh, :, cm] = stack([m1[j] for j in range(4)])
    xs = (1, 3, 2)
    q2 = [net.send(wq.at[y, xl, c, xh, :, col], net.dev(x=k)) for k in xs for col in (ca, cb)]
    m2 = [net.send(wm.at[y, xl, c, xh, :, cm], net.dev(x=k)) for k in xs]
    for cp in q2:
        cp.wait_recv()
    q3a = [net.send(wq.at[y, :, c, :, :, ca], net.dev(y=k)) for k in xs]
    q3b = [net.send(wq.at[y, :, c, :, :, cb], net.dev(z=k)) for k in xs]
    for cp in m2:
        cp.wait_recv()
    m3 = [net.send(wm.at[y, :, c, :, :, cm], net.dev(y=k)) for k in xs]
    for cp in q3a:
        cp.wait_recv()
    q4a = [net.send(wq.at[:, :, c, :, :, ca], net.dev(z=k)) for k in xs]
    for cp in q3b:
        cp.wait_recv()
    cbb = pl.ds(1024, 1024)
    q4b = [net.send(wq.at[y, :, c, :, :, cbb], net.dev(y=k)) for k in xs]
    q5 = [
        net.send(wq.at[:, :, c, :, :, ca], net.dev(c=1)),
        net.send(wq.at[y, :, c, :, :, cbb], net.dev(c=1)),
    ]
    sent += q2 + m2 + q3a + q3b + m3 + q4a + q4b
    for k in range(1, 8):
        first["e", k].wait_recv()

    def lay(src, dst, rows, width):
        def step(i, carry):
            col = pl.ds(pl.multiple_of(i * width, width), width)
            for e in range(2):
                dst[e, y, xl, c, :, col] = stack([src[j, e, :, col] for j in range(8)])
            return carry

        lax.fori_loop(0, D // width, step, 0)

    lay(e1, wi, 96, 256)
    i1 = net.send(wi.at[:, y, xl, c], net.xflip())
    i2 = {k: net.send(wi.at[:, y, xl, c], net.dev(y=k)) for k in (1, 3)}
    for k in range(1, 8):
        first["o", k].wait_recv()
    lay(o1, wo, 48, 256)
    u1 = {k: net.send(wo.at[:, y, xl, c], net.dev(y=k)) for k in (1, 3, 2)}
    p5 = [net.send(wi.at[:, y, xl, c], net.dev(c=1)), net.send(wo.at[:, y, xl, c], net.dev(c=1))]
    u2 = [net.send(wo.at[:, y, xl, c], net.xflip())]
    sent += [i1, *i2.values(), *u1.values(), *p5, *u2]
    for cp in m3:
        cp.wait_recv()
    m4 = [net.send(wm.at[:, :, c, :, :, cm], net.dev(z=k)) for k in xs]
    m5 = [net.send(wm.at[:, :, c, :, :, cm], net.dev(c=1))]
    sent += m4
    i1.wait_recv()
    i3 = {k: net.send(wi.at[:, y, 1 - xl, c], net.dev(y=k)) for k in (1, 3)}
    p5b = [net.send(wi.at[:, y, 1 - xl, c], net.dev(c=1))]
    sent += [*i3.values(), *p5b]
    for n, k in enumerate(xs):
        q4a[n].wait_recv()
        zf = (z + 4 - k) % 4
        q5.append(
            net.send(
                wq.at[:, :, c, :, :, pl.ds(pl.multiple_of(zf * 256, 256), 256)], net.dev(c=1)
            )
        )
        q4b[n].wait_recv()
        q5.append(net.send(wq.at[(y + 4 - k) % 4, :, c, :, :, cbb], net.dev(c=1)))
    sent += q5
    recv = list(q5)
    up, down = net.dev(y=1), net.dev(y=3)
    lo, hi = (y + 3) % 4, (y + 1) % 4
    for k in (1, 3):
        i2[k].wait_recv()
    for k in (1, 3):
        i3[k].wait_recv()
    r4 = [net.send(wi.at[:, lo, 0, c], up), net.send(wi.at[:, hi, 1, c], down)]
    p6 = [net.send(wi.at[:, lo, :, c], net.dev(c=1)), net.send(wi.at[:, hi, :, c], net.dev(c=1))]
    for n, k in enumerate(xs):
        u1[k].wait_recv()
        yf = (y + 4 - k) % 4
        u2.append(net.send(wo.at[:, yf, xl, c], net.xflip()))
        p6.append(net.send(wo.at[:, yf, xl, c], net.dev(c=1)))
        sent += u2[-1:]
    for n, k in enumerate(xs):
        m4[n].wait_recv()
        zf = (z + 4 - k) % 4
        m5.append(
            net.send(
                wm.at[:, :, c, :, :, pl.ds(pl.multiple_of(zf * 384, 128), 384)], net.dev(c=1)
            )
        )
    sent += m5
    recv += m5
    for n, k in enumerate((0,) + xs):
        u2[n].wait_recv()
        p6.append(net.send(wo.at[:, (y + 4 - k) % 4, 1 - xl, c], net.dev(c=1)))
    for cp in r4:
        cp.wait_recv()
    p6.append(net.send(wi.at[:, (y + 2) % 4, :, c], net.dev(c=1)))
    sent += r4 + p6
    recv += p5 + p5b + p6
    for cp in recv:
        cp.wait_recv()
    for (name, k), cp in first.items():
        if k:
            cp.wait_send()
        else:

            @pl.when(half != xh)
            def _(cp=cp):
                cp.wait_send()

    for cp in sent:
        cp.wait_send()


def weights_kernel(qs, ms, es, os, wq, wm, wi, wo, q1, m1, e1, o1, ss, rs):
    net = Net(ss, rs)
    enter(net)
    gather_weights(net, qs, ms, es, os, q1, m1, e1, o1, wq, wm, wi, wo)


def weights_call(qs, ms, es, os):
    vm = pl.BlockSpec(memory_space=pltpu.VMEM)
    return pl.pallas_call(
        weights_kernel,
        out_shape=(
            jax.ShapeDtypeStruct((4, 2, 2, 2, 48, 2048), BF),
            jax.ShapeDtypeStruct((4, 2, 2, 2, 48, D), BF),
            jax.ShapeDtypeStruct((2, 4, 2, 2, 96, D), BF),
            jax.ShapeDtypeStruct((2, 4, 2, 2, 48, D), BF),
        ),
        in_specs=[vm] * 4,
        out_specs=(vm,) * 4,
        scratch_shapes=[
            pltpu.VMEM((4, 12, 512), BF),
            pltpu.VMEM((4, 12, 384), BF),
            pltpu.VMEM((8, 2, 12, D), BF),
            pltpu.VMEM((8, 2, 6, D), BF),
            pltpu.SemaphoreType.DMA((120,)),
            pltpu.SemaphoreType.DMA((120,)),
        ],
        compiler_params=pltpu.CompilerParams(
            collective_id=0, has_side_effects=True, vmem_limit_bytes=60 << 20
        ),
    )(qs, ms, es, os)


def body(
    tokens,
    attn_in,
    attn_out,
    expert_in,
    expert_out,
    attn_gain,
    moe_gain,
    lengths,
    page_table,
    routes,
    gates,
):
    count = tokens.shape[0]
    cycle_size = lax.axis_size("blk")
    place = lax.axis_index("blk")
    group_rows = count * cycle_size
    local_experts = E // cycle_size
    heads_per = QH // KVH
    qs = attn_in.astype(BF).reshape(12, 2, 4, 256).transpose(2, 0, 1, 3).reshape(4, 12, 512)
    ms = attn_out.astype(BF).reshape(12, 4, 384).transpose(1, 0, 2)
    wq, wm, wi, wo = weights_call(qs, ms, expert_in.astype(BF), expert_out.astype(BF))
    wq, wm = wq.reshape(D, 2048), wm.reshape(D, D)
    wi, wo = wi.reshape(2, D, D), wo.reshape(2, FF, D)
    segment_all, position_all = segment_info(lengths[0], group_rows)
    first = place * count
    my_index = first + jnp.arange(count, dtype=jnp.int32)
    my_segment = lax.dynamic_slice_in_dim(segment_all, first, count)
    my_position = lax.dynamic_slice_in_dim(position_all, first, count).astype(jnp.float32)
    normed = rms_scale(tokens, attn_gain).astype(jnp.bfloat16)
    projected = jnp.dot(normed, wq, preferred_element_type=jnp.float32)
    queries = rotate(projected[:, :QW].reshape(count, QH, HD), my_position).astype(jnp.bfloat16)
    keys_here = rotate(
        projected[:, QW : QW + KVH * HD].reshape(count, KVH, HD), my_position
    ).astype(jnp.bfloat16)
    values_here = projected[:, QW + KVH * HD :].astype(jnp.bfloat16)
    cache_here = jnp.concatenate([keys_here.reshape(count, KVH * HD), values_here], axis=1)
    cache_all = lax.all_gather(cache_here, "blk", axis=0, tiled=True)
    keys_all = cache_all[:, : KVH * HD].reshape(group_rows, KVH, HD)
    values_all = cache_all[:, KVH * HD :].reshape(group_rows, KVH, HD)
    grouped = queries.reshape(count, KVH, heads_per, HD)
    scores = jnp.einsum(
        "igrd,jgd->grij", grouped, keys_all, preferred_element_type=jnp.float32
    ) / math.sqrt(HD)
    key_index = jnp.arange(group_rows, dtype=jnp.int32)
    allowed = (my_segment[:, None] == segment_all[None, :]) & (
        key_index[None, :] <= my_index[:, None]
    )
    scores = jnp.where(allowed[None, None], scores, jnp.float32(-1e30))
    highest = jnp.max(scores, axis=-1, keepdims=True)
    weights = jnp.exp(scores - highest)
    probs = (weights / jnp.sum(weights, axis=-1, keepdims=True)).astype(jnp.bfloat16)
    attended = jnp.einsum("grij,jgd->igrd", probs, values_all, preferred_element_type=jnp.float32)
    attended = attended.astype(jnp.bfloat16).reshape(count, QW)
    hidden = tokens.astype(jnp.float32) + jnp.dot(
        attended, wm, preferred_element_type=jnp.float32
    )
    page_count = count // PAGE
    targets = place * page_count + jnp.arange(page_count, dtype=jnp.int32)
    table = page_table[0]
    logical = jnp.sum(
        jnp.where(
            table[None, :] == targets[:, None],
            jnp.arange(table.shape[0], dtype=jnp.int32)[None, :],
            0,
        ),
        axis=1,
    )
    row_ids = logical[:, None] * PAGE + jnp.arange(PAGE, dtype=jnp.int32)[None, :]
    kv_pages = cache_all[row_ids]
    normed_two = rms_scale(hidden, moe_gain).astype(jnp.bfloat16)
    expert_ids = jnp.arange(E, dtype=jnp.int32)
    dense = jnp.sum(
        jnp.where(
            routes[:, :, None] == expert_ids[None, None, :],
            gates.astype(jnp.float32)[:, :, None],
            jnp.float32(0.0),
        ),
        axis=1,
    ).astype(jnp.bfloat16)
    rows_all, weight_all = (
        lax.all_gather(normed_two, "blk", axis=0, tiled=True),
        lax.all_gather(dense, "blk", axis=0, tiled=True),
    )
    owned_weight = lax.dynamic_slice_in_dim(weight_all, place * local_experts, local_experts, 1)
    owned_weight = owned_weight.reshape(cycle_size, count, local_experts)
    onehot, gated = jax.vmap(functools.partial(slot_tables, depth=CAP), in_axes=0, out_axes=1)(
        owned_weight
    )
    chosen = jnp.einsum(
        "jsct,stm->jscm",
        onehot,
        rows_all.reshape(cycle_size, count, D),
        preferred_element_type=jnp.float32,
    ).astype(jnp.bfloat16)
    section = chosen.reshape(local_experts, cycle_size * CAP, D)
    gate_up = jnp.einsum("erd,edf->erf", section, wi, preferred_element_type=jnp.float32)
    activated = (jax.nn.relu(gate_up[..., :FF]) * gate_up[..., FF:]).astype(jnp.bfloat16)
    summed = jnp.einsum("erf,efd->erd", activated, wo, preferred_element_type=jnp.float32)
    results = summed.astype(jnp.bfloat16)
    results = results.reshape(local_experts, cycle_size, CAP, D)
    summed = jnp.einsum("jsct,jscm->stm", gated, results, preferred_element_type=jnp.float32)
    expert_term = lax.psum_scatter(
        summed.reshape(count * lax.axis_size("blk"), D).astype(jnp.bfloat16),
        "blk",
        scatter_dimension=0,
        tiled=True,
    ).astype(jnp.float32)
    mixed = (hidden + expert_term).astype(jnp.bfloat16)
    return (mixed, kv_pages)


def solution(mesh):
    in_specs = (
        P(("rep", "blk"), None),
        P(("rep", "blk"), None),
        P(("rep", "blk"), None),
        P(None, ("rep", "blk"), None),
        P(None, ("rep", "blk"), None),
        P(),
        P(),
        P("rep", None),
        P("rep", None),
        P(("rep", "blk"), None),
        P(("rep", "blk"), None),
    )
    out_specs = (P(("rep", "blk"), None), P(("rep", "blk"), None, None))
    return jax.shard_map(body, mesh=mesh, in_specs=in_specs, out_specs=out_specs, check_vma=False)
```

```python
import math

import jax
import jax.numpy as jnp
from jax import lax
from jax.experimental import pallas as pl
from jax.experimental.pallas import tpu as pltpu
from jax.sharding import PartitionSpec as P

D = 1536
FF = 768
QH = 12
KVH = 2
HD = 128
E = 16
PAGE = 128
CAP = 64
QW = 1536
BF = jnp.bfloat16
F32 = jnp.float32
MESH = pl.DeviceIdType.MESH


class Net:
    def __init__(self, send_sems, recv_sems):
        rep, blk = lax.axis_index("rep"), lax.axis_index("blk")
        self.y, self.xl, self.c = rep // 4, (rep // 2) % 2, rep % 2
        self.z, self.xh = blk // 2, blk % 2
        self.x = self.xh * 2 + self.xl
        self.ss, self.rs, self.used = send_sems, recv_sems, 0

    def dev(self, y=0, x=0, z=0, c=0):
        yy = (self.y + y) % 4
        xx = (self.x + x) % 4
        zz = (self.z + z) % 4
        cc = (self.c + c) % 2
        return ((yy * 2 + xx % 2) * 2 + cc, zz * 2 + xx // 2)

    def xflip(self):
        return (((self.y * 2 + 1 - self.xl) * 2) + self.c, self.z * 2 + self.xh)

    def take(self, n=1):
        k = self.used
        self.used = k + n
        return k

    def make(self, src, dst, to, k):
        return pltpu.make_async_remote_copy(
            src_ref=src,
            dst_ref=dst,
            send_sem=self.ss.at[k],
            recv_sem=self.rs.at[k],
            device_id=to,
            device_id_type=MESH,
        )

    def send(self, ref, to):
        cp = self.make(ref, ref, to, self.take())
        cp.start()
        return cp


def enter(net):
    barrier = pltpu.get_barrier_semaphore()
    around = [net.dev(x=1), net.dev(x=3), net.dev(c=1)]
    around += [net.dev(y=k) for k in (1, 2, 3)]
    around += [net.dev(z=dz, x=dx) for dz in range(4) for dx in (0, 2) if dz or dx]
    for to in around:
        pl.semaphore_signal(barrier, inc=1, device_id=to, device_id_type=MESH)
    pl.semaphore_wait(barrier, len(around))


def scaled(values, gain):
    mean_sq = jnp.mean(values * values, axis=-1, keepdims=True)
    return (values * lax.rsqrt(mean_sq + 1e-06) * gain).astype(BF)


def stack(pieces):
    return jnp.concatenate([p.astype(F32) for p in pieces], axis=0).astype(BF)


def layer_kernel(
    qs,
    ms,
    es,
    os,
    wts,
    tokens,
    gain_a,
    gain_m,
    lengths,
    table,
    mixed,
    pages,
    wq,
    wm,
    wi,
    wo,
    q1,
    m1,
    e1,
    o1,
    wt,
    xn,
    qh,
    kv,
    at,
    hid,
    rows,
    oh,
    ga,
    msk,
    ch,
    act,
    res,
    pa,
    pb,
    ra,
    rb,
    rx,
    rz,
    ss,
    rs,
):
    net = Net(ss, rs)
    y, xl, c, z, xh = net.y, net.xl, net.c, net.z, net.xh
    blk = z * 2 + xh
    sent = []

    def send(ref, to, dst=None):
        cp = net.make(ref, ref if dst is None else dst, to, net.take())
        cp.start()
        sent.append(cp)
        return cp

    def blk_dev(b):
        return ((y * 2 + xl) * 2 + c, b)

    enter(net)
    half = z // 2
    slot = (z % 2) * 2 + xh
    first = {}
    for name, src, dst in (("q", qs, q1), ("m", ms, m1)):
        base = net.take(4)
        for k in range(4):
            zt = (z + k) % 4
            cp = pltpu.make_async_remote_copy(
                src_ref=src.at[zt],
                dst_ref=dst.at[slot],
                send_sem=ss.at[base + k],
                recv_sem=rs.at[base + slot],
                device_id=((y * 2 + xl) * 2 + c, zt * 2 + half),
                device_id_type=MESH,
            )
            first[name, k] = cp
            if k:
                cp.start()
                continue

            @pl.when(half != xh)
            def _(cp=cp):
                cp.start()

            @pl.when(half == xh)
            def _(src=src, dst=dst):
                dst[pl.ds(slot, 1)] = src[pl.ds(z, 1)]

    for name, src, dst, per in (("e", es, e1, 2), ("o", os, o1, 2), ("w", wts, wt, 1)):
        base = net.take(8)
        for k in range(1, 8):
            to = (blk + k) % 8
            part = src.at[pl.ds(2 * to, 2)] if per == 2 else src.at[to]
            cp = pltpu.make_async_remote_copy(
                src_ref=part,
                dst_ref=dst.at[blk],
                send_sem=ss.at[base + k],
                recv_sem=rs.at[base + k],
                device_id=blk_dev(to),
                device_id_type=MESH,
            )
            cp.start()
            first[name, k] = cp
        if per == 2:
            dst[pl.ds(blk, 1)] = src[pl.ds(2 * blk, 2)][None]
        else:
            dst[pl.ds(blk, 1)] = src[pl.ds(blk, 1)]

    tok = tokens[...].astype(F32)
    xn[...] = scaled(tok, gain_a[...])
    start_of = []
    total = jnp.int32(0)
    for i in range(6):
        start_of.append(total)
        total = total + lengths[0, i]

    def segment(index):
        seg = jnp.zeros_like(index)
        begin = jnp.zeros_like(index)
        for s in start_of[1:]:
            seg = seg + (index >= s).astype(jnp.int32)
            begin = jnp.where(index >= s, s, begin)
        return seg, begin

    low = jnp.maximum(blk - 4, 0)
    mine = lax.broadcasted_iota(jnp.int32, (128, 1), 0) + blk * 128
    my_seg, my_begin = segment(mine)
    key_at = lax.broadcasted_iota(jnp.int32, (1, 640), 1) + low * 128
    key_seg, _ = segment(key_at)
    msk[...] = jnp.where((my_seg == key_seg) & (key_at <= mine), 1.0, 0.0).astype(F32)
    lane = lax.broadcasted_iota(jnp.int32, (1, 128), 1)
    step = (lane % 64).astype(F32)
    frequency = jnp.exp(step * (-2.0 * math.log(10000.0) / 128))
    angle = (mine - my_begin).astype(F32) * frequency
    cosine = jnp.cos(angle)
    sine = jnp.where(lane < 64, -jnp.sin(angle), jnp.sin(angle))

    def wait_first(src, dst, base):
        for j in range(4):
            own = (z == 2 * xh + j // 2) & (xh == j % 2)

            @pl.when(jnp.logical_not(own))
            def _(j=j):
                net.make(src.at[0], dst.at[0], net.dev(c=1), base + j).wait_recv()

    wait_first(qs, q1, 0)
    block = stack([q1[j] for j in range(4)])
    ca = pl.ds(pl.multiple_of(z * 256, 256), 256)
    cb = pl.ds(pl.multiple_of(1024 + z * 256, 256), 256)
    cm = pl.ds(pl.multiple_of(z * 384, 128), 384)
    wq[y, xl, c, xh, :, ca] = block[:, :256]
    wq[y, xl, c, xh, :, cb] = block[:, 256:]
    wait_first(ms, m1, 4)
    wm[y, xl, c, xh, :, cm] = stack([m1[j] for j in range(4)])
    xs = (1, 3, 2)
    q2 = [send(wq.at[y, xl, c, xh, :, col], net.dev(x=k)) for k in xs for col in (ca, cb)]
    m2 = [send(wm.at[y, xl, c, xh, :, cm], net.dev(x=k)) for k in xs]

    for k in range(1, 8):
        first["w", k].wait_recv()
    upper = (
        lax.broadcasted_iota(jnp.int32, (128, 128), 0)
        <= lax.broadcasted_iota(jnp.int32, (128, 128), 1)
    )
    upper = jnp.where(upper, 1.0, 0.0).astype(BF)
    slots = lax.broadcasted_iota(jnp.int32, (64, 128), 0).astype(F32)

    def tables(s, carry):
        w = wt[s]
        member = jnp.where(w > 0, 1.0, 0.0)
        rank = jnp.dot(member.astype(BF), upper, preferred_element_type=F32) - 1.0
        for e in range(2):
            hit = (member[e : e + 1] > 0) & (rank[e : e + 1] == slots)
            oh[s, e * 64 : e * 64 + 64] = jnp.where(hit, 1.0, 0.0).astype(BF)
            ga[s, e * 64 : e * 64 + 64] = jnp.where(hit, w[e : e + 1], 0.0).astype(BF)
        return carry

    lax.fori_loop(0, 8, tables, 0)

    for cp in q2:
        cp.wait_recv()
    q3a = [send(wq.at[y, :, c, :, :, ca], net.dev(y=k)) for k in xs]
    q3b = [send(wq.at[y, :, c, :, :, cb], net.dev(z=k)) for k in xs]
    for cp in m2:
        cp.wait_recv()
    m3 = [send(wm.at[y, :, c, :, :, cm], net.dev(y=k)) for k in xs]
    for cp in q3a:
        cp.wait_recv()
    q4a = [send(wq.at[:, :, c, :, :, ca], net.dev(z=k)) for k in xs]
    for cp in q3b:
        cp.wait_recv()
    cbb = pl.ds(1024, 1024)
    q4b = [send(wq.at[y, :, c, :, :, cbb], net.dev(y=k)) for k in xs]
    q5 = [
        send(wq.at[:, :, c, :, :, ca], net.dev(c=1)),
        send(wq.at[y, :, c, :, :, cbb], net.dev(c=1)),
    ]
    for k in range(1, 8):
        first["e", k].wait_recv()

    def lay(src, dst, width):
        def one(i, carry):
            col = pl.ds(pl.multiple_of(i * width, width), width)
            for e in range(2):
                dst[e, y, xl, c, :, col] = stack([src[j, e, :, col] for j in range(8)])
            return carry

        lax.fori_loop(0, D // width, one, 0)

    lay(e1, wi, 256)
    i1 = send(wi.at[:, y, xl, c], net.xflip())
    i2 = {k: send(wi.at[:, y, xl, c], net.dev(y=k)) for k in (1, 3)}
    for k in range(1, 8):
        first["o", k].wait_recv()
    lay(o1, wo, 256)
    u1 = {k: send(wo.at[:, y, xl, c], net.dev(y=k)) for k in xs}
    p5 = [send(wi.at[:, y, xl, c], net.dev(c=1)), send(wo.at[:, y, xl, c], net.dev(c=1))]
    u2 = [send(wo.at[:, y, xl, c], net.xflip())]
    for cp in m3:
        cp.wait_recv()
    m4 = [send(wm.at[:, :, c, :, :, cm], net.dev(z=k)) for k in xs]
    m5 = [send(wm.at[:, :, c, :, :, cm], net.dev(c=1))]
    i1.wait_recv()
    i3 = {k: send(wi.at[:, y, 1 - xl, c], net.dev(y=k)) for k in (1, 3)}
    p5 += [send(wi.at[:, y, 1 - xl, c], net.dev(c=1))]
    for n, k in enumerate(xs):
        q4a[n].wait_recv()
        zf = (z + 4 - k) % 4
        col = pl.ds(pl.multiple_of(zf * 256, 256), 256)
        q5.append(send(wq.at[:, :, c, :, :, col], net.dev(c=1)))
        q4b[n].wait_recv()
        q5.append(send(wq.at[(y + 4 - k) % 4, :, c, :, :, cbb], net.dev(c=1)))
    for cp in q5:
        cp.wait_recv()

    def project(col):
        w = wq[:, :, :, :, :, col].reshape(D, 256)
        return jnp.dot(xn[...], w, preferred_element_type=F32)

    def turned(head):
        return (head * cosine + pltpu.roll(head, 64, 1) * sine).astype(BF)

    kk = project(pl.ds(1536, 256))
    vv = project(pl.ds(1792, 256))
    kv[pl.ds(blk, 1), :, pl.ds(0, 128)] = turned(kk[:, :128])[None]
    kv[pl.ds(blk, 1), :, pl.ds(128, 128)] = turned(kk[:, 128:])[None]
    kv[pl.ds(blk, 1), :, pl.ds(256, 256)] = vv.astype(BF)[None]
    kvs = [send(kv.at[blk], blk_dev((blk + k) % 8)) for k in range(1, 8)]

    def query(n, carry):
        p = project(pl.ds(pl.multiple_of(n * 256, 256), 256))
        qh[pl.ds(2 * n, 1)] = turned(p[:, :128])[None]
        qh[pl.ds(2 * n + 1, 1)] = turned(p[:, 128:])[None]
        return carry

    lax.fori_loop(0, 6, query, 0)
    up, down = net.dev(y=1), net.dev(y=3)
    lo, hi = (y + 3) % 4, (y + 1) % 4
    for cp in kvs:
        cp.wait_recv()
    pages[...] = kv[table[0, 0]]

    def attend(h, carry):
        g = h // 6
        k = kv[pl.ds(low, 5), :, pl.ds(pl.multiple_of(g * 128, 128), 128)].reshape(640, 128)
        v = kv[pl.ds(low, 5), :, pl.ds(pl.multiple_of(256 + g * 128, 128), 128)].reshape(640, 128)
        s = lax.dot_general(qh[h], k, (((1,), (1,)), ((), ())), preferred_element_type=F32)
        s = jnp.where(msk[...] > 0, s * (1.0 / math.sqrt(HD)), -1e30)
        w = jnp.exp(s - jnp.max(s, axis=-1, keepdims=True))
        p = (w / jnp.sum(w, axis=-1, keepdims=True)).astype(BF)
        a = jnp.dot(p, v, preferred_element_type=F32)
        at[:, pl.ds(pl.multiple_of(h * 128, 128), 128)] = a.astype(BF)
        return carry

    lax.fori_loop(0, 12, attend, 0)
    for n, k in enumerate(xs):
        m4[n].wait_recv()
        zf = (z + 4 - k) % 4
        col = pl.ds(pl.multiple_of(zf * 384, 128), 384)
        m5.append(send(wm.at[:, :, c, :, :, col], net.dev(c=1)))
    for k in (1, 3):
        i2[k].wait_recv()
    for k in (1, 3):
        i3[k].wait_recv()
    r4 = [send(wi.at[:, lo, 0, c], up), send(wi.at[:, hi, 1, c], down)]
    p6 = [send(wi.at[:, lo, :, c], net.dev(c=1)), send(wi.at[:, hi, :, c], net.dev(c=1))]
    for cp in m5:
        cp.wait_recv()

    def mix(n, carry):
        col = pl.ds(pl.multiple_of(n * 256, 256), 256)
        w = wm[:, :, :, :, :, col].reshape(D, 256)
        hid[:, col] = tokens[:, col].astype(F32) + jnp.dot(
            at[...], w, preferred_element_type=F32
        )
        return carry

    lax.fori_loop(0, 6, mix, 0)
    rows[pl.ds(blk, 1)] = scaled(hid[...], gain_m[...])[None]
    across = net.dev(x=2)
    t1 = {k: send(rows.at[blk], net.dev(z=k)) for k in xs}
    tx = send(rows.at[blk], across)

    for k in xs:
        u1[k].wait_recv()
        yf = (y + 4 - k) % 4
        u2.append(send(wo.at[:, yf, xl, c], net.xflip()))
        p6.append(send(wo.at[:, yf, xl, c], net.dev(c=1)))
    for n, k in enumerate((0,) + xs):
        u2[n].wait_recv()
        p6.append(send(wo.at[:, (y + 4 - k) % 4, 1 - xl, c], net.dev(c=1)))
    for cp in r4:
        cp.wait_recv()
    p6.append(send(wi.at[:, (y + 2) % 4, :, c], net.dev(c=1)))
    tx.wait_recv()
    blk_x = z * 2 + 1 - xh
    t2 = {k: send(rows.at[blk_x], net.dev(z=k)) for k in (1, 3)}
    t1[2].wait_recv()
    blk_o = ((z + 2) % 4) * 2 + xh
    t3 = send(rows.at[blk_o], across)
    for k in (1, 3):
        t1[k].wait_recv()
    for cp in p5 + p6:
        cp.wait_recv()

    order = (0, 1, 3, 2)

    def experts(plane, out):
        for j, dz in enumerate(order):
            s = ((z + dz) % 4) * 2 + plane

            def pick(n, carry, s=s, j=j):
                col = pl.ds(pl.multiple_of(n * 512, 512), 512)
                got = jnp.dot(oh[s], rows[s, :, col], preferred_element_type=F32).astype(BF)
                ch[0, j * 64 : j * 64 + 64, col] = got[:64]
                ch[1, j * 64 : j * 64 + 64, col] = got[64:]
                return carry

            lax.fori_loop(0, 3, pick, 0)

        def one(e, carry):
            def gate(n, carry):
                lo_col = pl.ds(pl.multiple_of(n * 256, 256), 256)
                up_col = pl.ds(pl.multiple_of(768 + n * 256, 256), 256)
                a = jnp.dot(
                    ch[e], wi[e, :, :, :, :, lo_col].reshape(D, 256), preferred_element_type=F32
                )
                b = jnp.dot(
                    ch[e], wi[e, :, :, :, :, up_col].reshape(D, 256), preferred_element_type=F32
                )
                act[:, lo_col] = (jnp.maximum(a, 0.0) * b).astype(BF)
                return carry

            lax.fori_loop(0, 3, gate, 0)

            def down_to(n, carry):
                col = pl.ds(pl.multiple_of(n * 256, 256), 256)
                r = jnp.dot(
                    act[...], wo[e, :, :, :, :, col].reshape(FF, 256), preferred_element_type=F32
                ).astype(BF)
                for j in range(4):
                    res[j, pl.ds(pl.multiple_of(e * 64, 64), 64), col] = r[j * 64 : j * 64 + 64]
                return carry

            lax.fori_loop(0, 6, down_to, 0)
            return carry

        lax.fori_loop(0, 2, one, 0)
        for j, dz in enumerate(order):
            s = ((z + dz) % 4) * 2 + plane

            def fold(n, carry, s=s, j=j, dz=dz):
                col = pl.ds(pl.multiple_of(n * 512, 512), 512)
                t = lax.dot_general(
                    ga[s], res[j, :, col], (((0,), (0,)), ((), ())), preferred_element_type=F32
                )
                if out is pa and dz == 0:
                    hid[:, col] = hid[:, col] + t
                else:
                    out[dz, :, col] = t.astype(BF)
                return carry

            lax.fori_loop(0, 3, fold, 0)

    experts(xh, pa)
    s1 = [send(pa.at[k], net.dev(z=k), ra.at[k // 2]) for k in (1, 3)]
    for cp in t2.values():
        cp.wait_recv()
    t3.wait_recv()
    experts(1 - xh, pb)
    s2 = [send(pb.at[2], across, rx.at[0])]
    s3 = [send(pb.at[k], net.dev(z=k), rb.at[k // 2]) for k in (1, 3)]
    for cp in s1:
        cp.wait_recv()
    hid[...] = hid[...] + ra[0].astype(F32) + ra[1].astype(F32)
    s2[0].wait_recv()
    pa[2] = (pa[2].astype(F32) + rx[0].astype(F32)).astype(BF)
    s4 = send(pa.at[2], net.dev(z=2), rz)
    for cp in s3:
        cp.wait_recv()
    pb[0] = (pb[0].astype(F32) + rb[0].astype(F32) + rb[1].astype(F32)).astype(BF)
    s5 = send(pb.at[0], across, rx.at[1])
    s4.wait_recv()
    s5.wait_recv()
    mixed[...] = (hid[...] + rz[...].astype(F32) + rx[1].astype(F32)).astype(BF)
    for (name, k), cp in first.items():
        if k:
            cp.wait_send()
        else:

            @pl.when(half != xh)
            def _(cp=cp):
                cp.wait_send()

    for cp in sent:
        cp.wait_send()


def layer_call(*args):
    vm = pl.BlockSpec(memory_space=pltpu.VMEM)
    sm = pl.BlockSpec(memory_space=pltpu.SMEM)
    return pl.pallas_call(
        layer_kernel,
        out_shape=(
            jax.ShapeDtypeStruct((128, D), BF),
            jax.ShapeDtypeStruct((128, 512), BF),
        ),
        in_specs=[vm] * 8 + [sm] * 2,
        out_specs=(vm,) * 2,
        scratch_shapes=[
            pltpu.VMEM((4, 2, 2, 2, 48, 2048), BF),
            pltpu.VMEM((4, 2, 2, 2, 48, D), BF),
            pltpu.VMEM((2, 4, 2, 2, 96, D), BF),
            pltpu.VMEM((2, 4, 2, 2, 48, D), BF),
            pltpu.VMEM((4, 12, 512), BF),
            pltpu.VMEM((4, 12, 384), BF),
            pltpu.VMEM((8, 2, 12, D), BF),
            pltpu.VMEM((8, 2, 6, D), BF),
            pltpu.VMEM((8, 2, 128), F32),
            pltpu.VMEM((128, D), BF),
            pltpu.VMEM((12, 128, 128), BF),
            pltpu.VMEM((8, 128, 512), BF),
            pltpu.VMEM((128, D), BF),
            pltpu.VMEM((128, D), F32),
            pltpu.VMEM((8, 128, D), BF),
            pltpu.VMEM((8, 128, 128), BF),
            pltpu.VMEM((8, 128, 128), BF),
            pltpu.VMEM((128, 640), F32),
            pltpu.VMEM((2, 256, D), BF),
            pltpu.VMEM((256, FF), BF),
            pltpu.VMEM((4, 128, D), BF),
            pltpu.VMEM((4, 128, D), BF),
            pltpu.VMEM((4, 128, D), BF),
            pltpu.VMEM((2, 128, D), BF),
            pltpu.VMEM((2, 128, D), BF),
            pltpu.VMEM((2, 128, D), BF),
            pltpu.VMEM((128, D), BF),
            pltpu.SemaphoreType.DMA((160,)),
            pltpu.SemaphoreType.DMA((160,)),
        ],
        compiler_params=pltpu.CompilerParams(
            collective_id=0, has_side_effects=True, vmem_limit_bytes=64 << 20
        ),
    )(*args)


def body(
    tokens,
    attn_in,
    attn_out,
    expert_in,
    expert_out,
    attn_gain,
    moe_gain,
    lengths,
    page_table,
    routes,
    gates,
):
    place = lax.axis_index("blk")
    qs = attn_in.astype(BF).reshape(12, 2, 4, 256).transpose(2, 0, 1, 3).reshape(4, 12, 512)
    ms = attn_out.astype(BF).reshape(12, 4, 384).transpose(1, 0, 2)
    ids = jnp.arange(E, dtype=jnp.int32)
    weight = jnp.sum(
        jnp.where(
            routes.T[None, :, :] == ids[:, None, None], gates.astype(F32).T[None, :, :], 0.0
        ),
        axis=1,
    ).reshape(8, 2, 128)
    page_ids = jnp.arange(8, dtype=jnp.int32)
    logical = jnp.sum(jnp.where(page_table == place, page_ids[None, :], 0), axis=1, keepdims=True)
    mixed, pages = layer_call(
        qs,
        ms,
        expert_in.astype(BF),
        expert_out.astype(BF),
        weight,
        tokens,
        attn_gain[None],
        moe_gain[None],
        lengths,
        logical,
    )
    return mixed, pages[None]


def solution(mesh):
    in_specs = (
        P(("rep", "blk"), None),
        P(("rep", "blk"), None),
        P(("rep", "blk"), None),
        P(None, ("rep", "blk"), None),
        P(None, ("rep", "blk"), None),
        P(),
        P(),
        P("rep", None),
        P("rep", None),
        P(("rep", "blk"), None),
        P(("rep", "blk"), None),
    )
    out_specs = (P(("rep", "blk"), None), P(("rep", "blk"), None, None))
    return jax.shard_map(body, mesh=mesh, in_specs=in_specs, out_specs=out_specs, check_vma=False)
```

```python
import math

import jax
import jax.numpy as jnp
from jax import lax
from jax.experimental import pallas as pl
from jax.experimental.pallas import tpu as pltpu
from jax.sharding import PartitionSpec as P

D = 1536
FF = 768
QH = 12
KVH = 2
HD = 128
E = 16
PAGE = 128
CAP = 64
QW = 1536
BF = jnp.bfloat16
F32 = jnp.float32
MESH = pl.DeviceIdType.MESH


class Net:
    def __init__(self, send_sems, recv_sems):
        rep, blk = lax.axis_index("rep"), lax.axis_index("blk")
        self.y, self.xl, self.c = rep // 4, (rep // 2) % 2, rep % 2
        self.z, self.xh = blk // 2, blk % 2
        self.x = self.xh * 2 + self.xl
        self.ss, self.rs, self.used = send_sems, recv_sems, 0

    def dev(self, y=0, x=0, z=0, c=0):
        yy = (self.y + y) % 4
        xx = (self.x + x) % 4
        zz = (self.z + z) % 4
        cc = (self.c + c) % 2
        return ((yy * 2 + xx % 2) * 2 + cc, zz * 2 + xx // 2)

    def xflip(self):
        return (((self.y * 2 + 1 - self.xl) * 2) + self.c, self.z * 2 + self.xh)

    def take(self, n=1):
        k = self.used
        self.used = k + n
        return k

    def make(self, src, dst, to, k):
        return pltpu.make_async_remote_copy(
            src_ref=src,
            dst_ref=dst,
            send_sem=self.ss.at[k],
            recv_sem=self.rs.at[k],
            device_id=to,
            device_id_type=MESH,
        )

    def send(self, ref, to):
        cp = self.make(ref, ref, to, self.take())
        cp.start()
        return cp


def enter(net):
    barrier = pltpu.get_barrier_semaphore()
    around = [net.dev(x=1), net.dev(x=3), net.dev(c=1)]
    around += [net.dev(y=k) for k in (1, 2, 3)]
    around += [net.dev(z=dz, x=dx) for dz in range(4) for dx in (0, 2) if dz or dx]
    for to in around:
        pl.semaphore_signal(barrier, inc=1, device_id=to, device_id_type=MESH)
    pl.semaphore_wait(barrier, len(around))


def scaled(values, gain):
    mean_sq = jnp.mean(values * values, axis=-1, keepdims=True)
    return (values * lax.rsqrt(mean_sq + 1e-06) * gain).astype(BF)


def stack(pieces):
    return jnp.concatenate([p.astype(F32) for p in pieces], axis=0).astype(BF)


def layer_kernel(
    xq,
    xm,
    xe,
    xo,
    tokens,
    wts,
    gain_a,
    gain_m,
    lengths,
    table,
    mixed,
    pages,
    wq,
    wm,
    wi,
    wo,
    fq,
    fm,
    fe,
    fo,
    tk,
    qs,
    ms,
    es,
    os,
    q1,
    m1,
    e1,
    o1,
    wt,
    xn,
    qh,
    kv,
    near,
    at,
    hid,
    rows,
    oh,
    ga,
    msk,
    ch,
    act,
    res,
    pa,
    pb,
    ra,
    rb,
    rx,
    rz,
    ls,
    ss,
    rs,
):
    net = Net(ss, rs)
    y, xl, c, z, xh = net.y, net.xl, net.c, net.z, net.xh
    blk = z * 2 + xh
    sent = []

    def send(ref, to, dst=None):
        cp = net.make(ref, ref if dst is None else dst, to, net.take())
        cp.start()
        sent.append(cp)
        return cp

    def blk_dev(b):
        return ((y * 2 + xl) * 2 + c, b)

    loads = []
    for n, (src, dst) in enumerate(
        ((xq, fq), (xm, fm), (tokens, tk), (xe, fe), (xo, fo))
    ):
        cp = pltpu.make_async_copy(src, dst, ls.at[n])
        cp.start()
        loads.append(cp)
    loads[0].wait()
    for k in range(4):
        qs[k, :, 0:128] = fq[:, k * 128 : k * 128 + 128].astype(BF)
        qs[k, :, 128:384] = fq[:, 512 + k * 256 : 768 + k * 256].astype(BF)
        qs[k, :, 384:512] = fq[:, 1536 + k * 128 : 1664 + k * 128].astype(BF)
    loads[1].wait()
    for k in range(4):
        ms[k, :, 0:128] = fm[:, k * 128 : k * 128 + 128].astype(BF)
        ms[k, :, 128:384] = fm[:, 512 + k * 256 : 768 + k * 256].astype(BF)
    enter(net)
    half = z // 2
    slot = (z % 2) * 2 + xh
    first = {}
    for name, src, dst in (("q", qs, q1), ("m", ms, m1)):
        base = net.take(4)
        for k in range(4):
            zt = (z + k) % 4
            cp = pltpu.make_async_remote_copy(
                src_ref=src.at[zt],
                dst_ref=dst.at[slot],
                send_sem=ss.at[base + k],
                recv_sem=rs.at[base + slot],
                device_id=((y * 2 + xl) * 2 + c, zt * 2 + half),
                device_id_type=MESH,
            )
            first[name, k] = cp
            if k:
                cp.start()
                continue

            @pl.when(half != xh)
            def _(cp=cp):
                cp.start()

            @pl.when(half == xh)
            def _(src=src, dst=dst):
                dst[pl.ds(slot, 1)] = src[pl.ds(z, 1)]

    def spread(name, src, dst):
        base = net.take(8)
        for k in range(1, 8):
            to = (blk + k) % 8
            cp = pltpu.make_async_remote_copy(
                src_ref=src.at[to],
                dst_ref=dst.at[blk],
                send_sem=ss.at[base + k],
                recv_sem=rs.at[base + k],
                device_id=blk_dev(to),
                device_id_type=MESH,
            )
            cp.start()
            first[name, k] = cp
        dst[pl.ds(blk, 1)] = src[pl.ds(blk, 1)]

    spread("w", wts, wt)
    loads[2].wait()
    tok = tk[...].astype(F32)
    xn[...] = scaled(tok, gain_a[...].reshape(1, D))
    start_of = []
    total = jnp.int32(0)
    for i in range(6):
        start_of.append(total)
        total = total + lengths[0, i]

    def segment(index):
        seg = jnp.zeros_like(index)
        begin = jnp.zeros_like(index)
        for s in start_of[1:]:
            seg = seg + (index >= s).astype(jnp.int32)
            begin = jnp.where(index >= s, s, begin)
        return seg, begin

    low = blk - 4
    for k in range(1, 5):

        @pl.when(blk < k)
        def _(k=k):
            near[4 - k] = jnp.zeros((128, 512), BF)

    mine = lax.broadcasted_iota(jnp.int32, (128, 1), 0) + blk * 128
    my_seg, my_begin = segment(mine)

    def wait_first(src, dst, base):
        for j in range(4):
            own = (z == 2 * xh + j // 2) & (xh == j % 2)

            @pl.when(jnp.logical_not(own))
            def _(j=j):
                net.make(src.at[0], dst.at[0], net.dev(c=1), base + j).wait_recv()

    def zcol(base, width, at):
        return pl.ds(pl.multiple_of(base + at * width, 128), width)

    xs = (1, 3, 2)

    class Color:
        def __init__(self, ref, base, width, axes):
            self.ref, self.base, self.width, self.axes = ref, base, width, axes
            self.stage, self.chip = 0, []

        def view(self, axes, **moved):
            at = {"y": y, "x": net.x, "z": z, **moved}
            yy = slice(None) if "y" in axes else at["y"]
            xx = slice(None) if "x" in axes else at["x"] % 2
            hh = slice(None) if "x" in axes else at["x"] // 2
            whole = pl.ds(self.base, 4 * self.width)
            cc = whole if "z" in axes else zcol(self.base, self.width, at["z"])
            return self.ref.at[yy, xx, c, hh, :, cc]

        def go(self):
            axis, done = self.axes[self.stage], self.axes[: self.stage]
            part = self.view(done)
            self.cps = [send(part, net.dev(**{axis: k})) for k in xs]
            self.stage += 1
            if self.stage == 3:
                self.chip.append(send(part, net.dev(c=1)))

        def arrive(self):
            for cp in self.cps:
                cp.wait_recv()

        def land(self, n):
            axis = self.axes[2]
            self.cps[n].wait_recv()
            here = {"y": y, "x": net.x, "z": z}[axis]
            got = self.view(self.axes[:2], **{axis: (here + 4 - xs[n]) % 4})
            self.chip.append(send(got, net.dev(c=1)))

        def close(self):
            for cp in self.chip:
                cp.wait_recv()

    qc = [Color(wq, 512, 256, "xzy"), Color(wq, 0, 128, "xyz"), Color(wq, 1536, 128, "yzx")]
    mc = [Color(wm, 512, 256, "yzx"), Color(wm, 0, 128, "xyz")]
    wait_first(qs, q1, 0)
    block = stack([q1[j] for j in range(4)])
    wq[y, xl, c, xh, :, zcol(0, 128, z)] = block[:, 0:128]
    wq[y, xl, c, xh, :, zcol(512, 256, z)] = block[:, 128:384]
    wq[y, xl, c, xh, :, zcol(1536, 128, z)] = block[:, 384:512]
    for q in qc:
        q.go()
    wait_first(ms, m1, 4)
    block = stack([m1[j] for j in range(4)])
    wm[y, xl, c, xh, :, zcol(0, 128, z)] = block[:, 0:128]
    wm[y, xl, c, xh, :, zcol(512, 256, z)] = block[:, 128:384]
    for m in mc:
        m.go()
    loads[3].wait()
    loads[4].wait()

    for d in range(8):
        es[d] = stack([fe[:, 2 * d], fe[:, 2 * d + 1]])
        os[d] = stack(
            [fo[:, 2 * d + i // 2, i % 2 * 768 : i % 2 * 768 + 768] for i in range(4)]
        )
    for q in qc:
        q.arrive()
        q.go()
    spread("e", es, e1)
    spread("o", os, o1)
    key_at = lax.broadcasted_iota(jnp.int32, (1, 640), 1) + low * 128
    key_seg, _ = segment(key_at)
    msk[...] = jnp.where((my_seg == key_seg) & (key_at <= mine) & (key_at >= 0), 1.0, 0.0).astype(F32)
    lane = lax.broadcasted_iota(jnp.int32, (1, 128), 1)
    step = (lane % 64).astype(F32)
    frequency = jnp.exp(step * (-2.0 * math.log(10000.0) / 128))
    angle = (mine - my_begin).astype(F32) * frequency
    cosine = jnp.cos(angle)
    sine = jnp.where(lane < 64, -jnp.sin(angle), jnp.sin(angle))
    for q in qc:
        q.arrive()
        q.go()
    for m in mc:
        m.arrive()
        m.go()
    for k in range(1, 8):
        first["w", k].wait_recv()
    upper = (
        lax.broadcasted_iota(jnp.int32, (128, 128), 0)
        <= lax.broadcasted_iota(jnp.int32, (128, 128), 1)
    )
    upper = jnp.where(upper, 1.0, 0.0).astype(BF)
    slots = lax.broadcasted_iota(jnp.int32, (64, 128), 0).astype(F32)

    def tables(s, carry):
        w = wt[s]
        member = jnp.where(w > 0, 1.0, 0.0)
        rank = jnp.dot(member.astype(BF), upper, preferred_element_type=F32) - 1.0
        for e in range(2):
            hit = (member[e : e + 1] > 0) & (rank[e : e + 1] == slots)
            oh[s, e * 64 : e * 64 + 64] = jnp.where(hit, 1.0, 0.0).astype(BF)
            ga[s, e * 64 : e * 64 + 64] = jnp.where(hit, w[e : e + 1], 0.0).astype(BF)
        return carry

    lax.fori_loop(0, 8, tables, 0)
    for k in range(1, 8):
        first["e", k].wait_recv()

    def lay_in(i, carry):
        col = pl.ds(pl.multiple_of(i * 256, 256), 256)
        got = [e1[j, :, col].astype(F32) for j in range(8)]
        for e in range(2):
            part = [g[e * 12 : e * 12 + 12] for g in got]
            wi[e, y, xl, c, :, col] = jnp.concatenate(part, axis=0).astype(BF)
        return carry

    def lay_out(i, carry):
        col = pl.ds(pl.multiple_of(i * 256, 256), 256)
        got = [o1[j, :, col].astype(F32) for j in range(8)]
        for n in range(4):
            part = [g[n * 6 : n * 6 + 6] for g in got]
            to = pl.ds(pl.multiple_of(n % 2 * 768 + i * 256, 256), 256)
            wo[n // 2, y, xl, c, :, to] = jnp.concatenate(part, axis=0).astype(BF)
        return carry

    lax.fori_loop(0, 6, lay_in, 0)
    i1 = [send(wi.at[:, y, xl, c], net.xflip())]
    i2 = {k: [send(wi.at[:, y, xl, c], net.dev(y=k))] for k in (1, 3)}
    for k in range(1, 8):
        first["o", k].wait_recv()
    lax.fori_loop(0, 3, lay_out, 0)
    i1.append(send(wo.at[:, y, xl, c], net.xflip()))
    for k in (1, 3):
        i2[k].append(send(wo.at[:, y, xl, c], net.dev(y=k)))
    for m in mc:
        m.arrive()
        m.go()
    for n in range(3):
        for q in qc:
            q.land(n)
    p5 = [send(w.at[:, y, xl, c], net.dev(c=1)) for w in (wi, wo)]
    for q in qc:
        q.close()

    def project(col):
        w = wq[:, :, :, :, :, col].reshape(D, 256)
        return jnp.dot(xn[...], w, preferred_element_type=F32)

    def turned(head):
        return (head * cosine + pltpu.roll(head, 64, 1) * sine).astype(BF)

    kk = project(pl.ds(1536, 256))
    vv = project(pl.ds(1792, 256))
    near[4, :, 0:128] = turned(kk[:, :128])
    near[4, :, 128:256] = turned(kk[:, 128:])
    near[4, :, 256:512] = vv.astype(BF)
    base = net.take(16)
    close_kv, far_kv = {}, {}
    for k in range(1, 8):
        to = blk_dev((blk + k) % 8)
        far_kv[k] = net.make(near.at[4], kv.at[blk], to, base + k)
        if k < 5:
            close_kv[k] = net.make(near.at[4], near.at[4 - k], to, base + 8 + k)

            @pl.when(blk + k < 8)
            def _(k=k):
                close_kv[k].start()


    def query(n, carry):
        p = project(pl.ds(pl.multiple_of(n * 256, 256), 256))
        qh[pl.ds(2 * n, 1)] = turned(p[:, :128])[None]
        qh[pl.ds(2 * n + 1, 1)] = turned(p[:, 128:])[None]
        return carry

    lax.fori_loop(0, 6, query, 0)
    for cp in i1:
        cp.wait_recv()
    i3 = {k: [send(w.at[:, y, 1 - xl, c], net.dev(y=k)) for w in (wi, wo)] for k in (1, 3)}
    p5 += [send(w.at[:, y, 1 - xl, c], net.dev(c=1)) for w in (wi, wo)]
    up, down = net.dev(y=1), net.dev(y=3)
    lo, hi = (y + 3) % 4, (y + 1) % 4
    for k in range(1, 5):

        @pl.when(blk >= k)
        def _(k=k):
            close_kv[k].wait_recv()


    def attend(h, carry):
        g = h // 6
        k = near[:, :, pl.ds(pl.multiple_of(g * 128, 128), 128)].reshape(640, 128)
        v = near[:, :, pl.ds(pl.multiple_of(256 + g * 128, 128), 128)].reshape(640, 128)
        s = lax.dot_general(qh[h], k, (((1,), (1,)), ((), ())), preferred_element_type=F32)
        s = jnp.where(msk[...] > 0, s * (1.0 / math.sqrt(HD)), -1e30)
        w = jnp.exp(s - jnp.max(s, axis=-1, keepdims=True))
        p = (w / jnp.sum(w, axis=-1, keepdims=True)).astype(BF)
        a = jnp.dot(p, v, preferred_element_type=F32)
        at[:, pl.ds(pl.multiple_of(h * 128, 128), 128)] = a.astype(BF)
        return carry

    lax.fori_loop(0, 12, attend, 0)
    for n in range(3):
        for m in mc:
            m.land(n)
    for m in mc:
        m.close()

    def mix(n, carry):
        col = pl.ds(pl.multiple_of(n * 256, 256), 256)
        w = wm[:, :, :, :, :, col].reshape(D, 256)
        hid[:, col] = tk[:, col].astype(F32) + jnp.dot(
            at[...], w, preferred_element_type=F32
        )
        return carry

    lax.fori_loop(0, 6, mix, 0)
    rows[pl.ds(blk, 1)] = scaled(hid[...], gain_m[...].reshape(1, D))[None]
    across = net.dev(x=2)
    t1 = {k: send(rows.at[blk], net.dev(z=k)) for k in xs}
    tx = send(rows.at[blk], across)

    for k in range(1, 8):
        if k > 4:
            far_kv[k].start()
            continue

        @pl.when(blk + k >= 8)
        def _(k=k):
            far_kv[k].start()

    for k in (1, 3):
        for cp in i2[k] + i3[k]:
            cp.wait_recv()
    r4 = [send(w.at[:, lo, 0, c], up) for w in (wi, wo)]
    r4 += [send(w.at[:, hi, 1, c], down) for w in (wi, wo)]
    p6 = [send(w.at[:, v, :, c], net.dev(c=1)) for w in (wi, wo) for v in (lo, hi)]
    tx.wait_recv()
    blk_x = z * 2 + 1 - xh
    t2 = {k: send(rows.at[blk_x], net.dev(z=k)) for k in (1, 3)}
    t1[2].wait_recv()
    blk_o = ((z + 2) % 4) * 2 + xh
    t3 = send(rows.at[blk_o], across)
    for k in (1, 3):
        t1[k].wait_recv()
    for cp in r4:
        cp.wait_recv()
    p6 += [send(w.at[:, (y + 2) % 4, :, c], net.dev(c=1)) for w in (wi, wo)]
    for cp in p5 + p6:
        cp.wait_recv()

    order = (0, 1, 3, 2)

    def experts(plane, out):
        for j, dz in enumerate(order):
            s = ((z + dz) % 4) * 2 + plane

            def pick(n, carry, s=s, j=j):
                col = pl.ds(pl.multiple_of(n * 512, 512), 512)
                got = jnp.dot(oh[s], rows[s, :, col], preferred_element_type=F32).astype(BF)
                ch[0, j * 64 : j * 64 + 64, col] = got[:64]
                ch[1, j * 64 : j * 64 + 64, col] = got[64:]
                return carry

            lax.fori_loop(0, 3, pick, 0)

        def one(e, carry):
            def gate(n, carry):
                lo_col = pl.ds(pl.multiple_of(n * 256, 256), 256)
                up_col = pl.ds(pl.multiple_of(768 + n * 256, 256), 256)
                a = jnp.dot(
                    ch[e], wi[e, :, :, :, :, lo_col].reshape(D, 256), preferred_element_type=F32
                )
                b = jnp.dot(
                    ch[e], wi[e, :, :, :, :, up_col].reshape(D, 256), preferred_element_type=F32
                )
                act[:, lo_col] = (jnp.maximum(a, 0.0) * b).astype(BF)
                return carry

            lax.fori_loop(0, 3, gate, 0)

            def down_to(n, carry):
                col = pl.ds(pl.multiple_of(n * 256, 256), 256)
                r = jnp.dot(
                    act[...], wo[e, :, :, :, :, col].reshape(FF, 256), preferred_element_type=F32
                ).astype(BF)
                for j in range(4):
                    res[j, pl.ds(pl.multiple_of(e * 64, 64), 64), col] = r[j * 64 : j * 64 + 64]
                return carry

            lax.fori_loop(0, 6, down_to, 0)
            return carry

        lax.fori_loop(0, 2, one, 0)
        for j, dz in enumerate(order):
            s = ((z + dz) % 4) * 2 + plane

            def fold(n, carry, s=s, j=j, dz=dz):
                col = pl.ds(pl.multiple_of(n * 512, 512), 512)
                t = lax.dot_general(
                    ga[s], res[j, :, col], (((0,), (0,)), ((), ())), preferred_element_type=F32
                )
                if out is pa and dz == 0:
                    hid[:, col] = hid[:, col] + t
                else:
                    out[dz, :, col] = t.astype(BF)
                return carry

            lax.fori_loop(0, 3, fold, 0)

    experts(xh, pa)
    s1 = [send(pa.at[k], net.dev(z=k), ra.at[k // 2]) for k in (1, 3)]
    for cp in t2.values():
        cp.wait_recv()
    t3.wait_recv()
    experts(1 - xh, pb)
    s2 = [send(pb.at[2], across, rx.at[0])]
    s3 = [send(pb.at[k], net.dev(z=k), rb.at[k // 2]) for k in (1, 3)]
    for cp in s1:
        cp.wait_recv()
    hid[...] = hid[...] + ra[0].astype(F32) + ra[1].astype(F32)
    s2[0].wait_recv()
    pa[2] = (pa[2].astype(F32) + rx[0].astype(F32)).astype(BF)
    s4 = send(pa.at[2], net.dev(z=2), rz)
    for cp in s3:
        cp.wait_recv()
    pb[0] = (pb[0].astype(F32) + rb[0].astype(F32) + rb[1].astype(F32)).astype(BF)
    s5 = send(pb.at[0], across, rx.at[1])
    kv[pl.ds(blk, 1)] = near[4][None]
    for k in range(1, 8):
        if k > 4:
            far_kv[k].wait_recv()
            far_kv[k].wait_send()
            continue

        @pl.when(blk < k)
        def _(k=k):
            far_kv[k].wait_recv()

        @pl.when(blk >= k)
        def _(k=k):
            kv[pl.ds(blk - k, 1)] = near[4 - k][None]

        @pl.when(blk + k < 8)
        def _(k=k):
            close_kv[k].wait_send()

        @pl.when(blk + k >= 8)
        def _(k=k):
            far_kv[k].wait_send()

    logical = jnp.int32(0)
    for i in range(8):
        logical = jnp.where(table[0, i] == blk, i, logical)
    pages[...] = kv[logical]
    s4.wait_recv()
    s5.wait_recv()
    mixed[...] = (hid[...] + rz[...].astype(F32) + rx[1].astype(F32)).astype(BF)
    for (name, k), cp in first.items():
        if k:
            cp.wait_send()
        else:

            @pl.when(half != xh)
            def _(cp=cp):
                cp.wait_send()

    for cp in sent:
        cp.wait_send()


def layer_call(*args):
    vm = pl.BlockSpec(memory_space=pltpu.VMEM)
    sm = pl.BlockSpec(memory_space=pltpu.SMEM)
    return pl.pallas_call(
        layer_kernel,
        out_shape=(
            jax.ShapeDtypeStruct((128, D), BF),
            jax.ShapeDtypeStruct((128, 512), BF),
        ),
        in_specs=[pl.BlockSpec(memory_space=pl.ANY)] * 5 + [vm] * 3 + [sm] * 2,
        out_specs=(vm,) * 2,
        scratch_shapes=[
            pltpu.VMEM((4, 2, 2, 2, 48, 2048), BF),
            pltpu.VMEM((4, 2, 2, 2, 48, D), BF),
            pltpu.VMEM((2, 4, 2, 2, 96, D), BF),
            pltpu.VMEM((2, 4, 2, 2, 48, D), BF),
            pltpu.VMEM((12, 2048), F32),
            pltpu.VMEM((12, D), F32),
            pltpu.VMEM((12, 16, D), F32),
            pltpu.VMEM((6, 16, D), F32),
            pltpu.VMEM((128, D), BF),
            pltpu.VMEM((4, 12, 512), BF),
            pltpu.VMEM((4, 12, 384), BF),
            pltpu.VMEM((8, 24, D), BF),
            pltpu.VMEM((8, 24, FF), BF),
            pltpu.VMEM((4, 12, 512), BF),
            pltpu.VMEM((4, 12, 384), BF),
            pltpu.VMEM((8, 24, D), BF),
            pltpu.VMEM((8, 24, FF), BF),
            pltpu.VMEM((8, 2, 128), F32),
            pltpu.VMEM((128, D), BF),
            pltpu.VMEM((12, 128, 128), BF),
            pltpu.VMEM((8, 128, 512), BF),
            pltpu.VMEM((5, 128, 512), BF),
            pltpu.VMEM((128, D), BF),
            pltpu.VMEM((128, D), F32),
            pltpu.VMEM((8, 128, D), BF),
            pltpu.VMEM((8, 128, 128), BF),
            pltpu.VMEM((8, 128, 128), BF),
            pltpu.VMEM((128, 640), F32),
            pltpu.VMEM((2, 256, D), BF),
            pltpu.VMEM((256, FF), BF),
            pltpu.VMEM((4, 128, D), BF),
            pltpu.VMEM((4, 128, D), BF),
            pltpu.VMEM((4, 128, D), BF),
            pltpu.VMEM((2, 128, D), BF),
            pltpu.VMEM((2, 128, D), BF),
            pltpu.VMEM((2, 128, D), BF),
            pltpu.VMEM((128, D), BF),
            pltpu.SemaphoreType.DMA((5,)),
            pltpu.SemaphoreType.DMA((200,)),
            pltpu.SemaphoreType.DMA((200,)),
        ],
        compiler_params=pltpu.CompilerParams(
            collective_id=0, has_side_effects=True, vmem_limit_bytes=64 << 20
        ),
    )(*args)


def body(
    tokens,
    attn_in,
    attn_out,
    expert_in,
    expert_out,
    attn_gain,
    moe_gain,
    lengths,
    page_table,
    routes,
    gates,
):
    ids = jnp.arange(E, dtype=jnp.int32)
    weight = jnp.sum(
        jnp.where(
            routes.T[None, :, :] == ids[:, None, None], gates.astype(F32).T[None, :, :], 0.0
        ),
        axis=1,
    ).reshape(8, 2, 128)
    mixed, pages = layer_call(
        attn_in,
        attn_out,
        expert_in.transpose(1, 0, 2),
        expert_out.transpose(1, 0, 2),
        tokens,
        weight,
        attn_gain,
        moe_gain,
        lengths,
        page_table,
    )
    return mixed, pages[None]


def solution(mesh):
    in_specs = (
        P(("rep", "blk"), None),
        P(("rep", "blk"), None),
        P(("rep", "blk"), None),
        P(None, ("rep", "blk"), None),
        P(None, ("rep", "blk"), None),
        P(),
        P(),
        P("rep", None),
        P("rep", None),
        P(("rep", "blk"), None),
        P(("rep", "blk"), None),
    )
    out_specs = (P(("rep", "blk"), None), P(("rep", "blk"), None, None))
    return jax.shard_map(body, mesh=mesh, in_specs=in_specs, out_specs=out_specs, check_vma=False)
```

```python
import math

import jax
import jax.numpy as jnp
from jax import lax
from jax.experimental import pallas as pl
from jax.experimental.pallas import tpu as pltpu
from jax.sharding import PartitionSpec as P

D = 1536
FF = 768
QH = 12
KVH = 2
HD = 128
E = 16
PAGE = 128
CAP = 64
QW = 1536
BF = jnp.bfloat16
F32 = jnp.float32
MESH = pl.DeviceIdType.MESH


class Net:
    def __init__(self, send_sems, recv_sems):
        rep, blk = lax.axis_index("rep"), lax.axis_index("blk")
        self.y, self.xl, self.c = rep // 4, (rep // 2) % 2, rep % 2
        self.z, self.xh = blk // 2, blk % 2
        self.x = self.xh * 2 + self.xl
        self.ss, self.rs, self.used = send_sems, recv_sems, 0

    def dev(self, y=0, x=0, z=0, c=0):
        yy = (self.y + y) % 4
        xx = (self.x + x) % 4
        zz = (self.z + z) % 4
        cc = (self.c + c) % 2
        return ((yy * 2 + xx % 2) * 2 + cc, zz * 2 + xx // 2)

    def xflip(self):
        return (((self.y * 2 + 1 - self.xl) * 2) + self.c, self.z * 2 + self.xh)

    def take(self, n=1):
        k = self.used
        self.used = k + n
        return k

    def make(self, src, dst, to, k):
        return pltpu.make_async_remote_copy(
            src_ref=src,
            dst_ref=dst,
            send_sem=self.ss.at[k],
            recv_sem=self.rs.at[k],
            device_id=to,
            device_id_type=MESH,
        )

    def send(self, ref, to):
        cp = self.make(ref, ref, to, self.take())
        cp.start()
        return cp


def enter(net):
    barrier = pltpu.get_barrier_semaphore()
    around = [net.dev(x=1), net.dev(x=3), net.dev(c=1)]
    around += [net.dev(y=k) for k in (1, 2, 3)]
    around += [net.dev(z=dz, x=dx) for dz in range(4) for dx in (0, 2) if dz or dx]
    for to in around:
        pl.semaphore_signal(barrier, inc=1, device_id=to, device_id_type=MESH)
    pl.semaphore_wait(barrier, len(around))


def scaled(values, gain):
    mean_sq = jnp.mean(values * values, axis=-1, keepdims=True)
    return (values * lax.rsqrt(mean_sq + 1e-06) * gain).astype(BF)


def stack(pieces):
    return jnp.concatenate([p.astype(F32) for p in pieces], axis=0).astype(BF)


def layer_kernel(
    xq,
    xm,
    xe,
    xo,
    tokens,
    wts,
    gain_a,
    gain_m,
    lengths,
    table,
    mixed,
    pages,
    wq,
    wm,
    wi,
    wo,
    fq,
    fm,
    fe,
    fo,
    tk,
    qs,
    ms,
    es,
    os,
    q1,
    m1,
    e1,
    o1,
    wt,
    xn,
    qh,
    kv,
    near,
    at,
    hid,
    rows,
    oh,
    ga,
    msk,
    ch,
    act,
    res,
    pa,
    pb,
    ra,
    rb,
    rx,
    rz,
    ls,
    ss,
    rs,
):
    net = Net(ss, rs)
    y, xl, c, z, xh = net.y, net.xl, net.c, net.z, net.xh
    blk = z * 2 + xh
    sent = []

    def send(ref, to, dst=None):
        cp = net.make(ref, ref if dst is None else dst, to, net.take())
        cp.start()
        sent.append(cp)
        return cp

    def blk_dev(b):
        return ((y * 2 + xl) * 2 + c, b)

    loads = []
    for n, (src, dst) in enumerate(
        ((xq, fq), (xm, fm), (tokens, tk), (xe, fe), (xo, fo))
    ):
        cp = pltpu.make_async_copy(src, dst, ls.at[n])
        cp.start()
        loads.append(cp)
    loads[0].wait()
    for k in range(4):
        qs[k, :, 0:128] = fq[:, k * 128 : k * 128 + 128].astype(BF)
        qs[k, :, 128:384] = fq[:, 512 + k * 256 : 768 + k * 256].astype(BF)
        qs[k, :, 384:512] = fq[:, 1536 + k * 128 : 1664 + k * 128].astype(BF)
    loads[1].wait()
    for k in range(4):
        ms[k, :, 0:128] = fm[:, k * 128 : k * 128 + 128].astype(BF)
        ms[k, :, 128:384] = fm[:, 512 + k * 256 : 768 + k * 256].astype(BF)
    enter(net)
    half = z // 2
    slot = (z % 2) * 2 + xh
    first = {}
    for name, src, dst in (("q", qs, q1), ("m", ms, m1)):
        base = net.take(4)
        for k in range(4):
            zt = (z + k) % 4
            cp = pltpu.make_async_remote_copy(
                src_ref=src.at[zt],
                dst_ref=dst.at[slot],
                send_sem=ss.at[base + k],
                recv_sem=rs.at[base + slot],
                device_id=((y * 2 + xl) * 2 + c, zt * 2 + half),
                device_id_type=MESH,
            )
            first[name, k] = cp
            if k:
                cp.start()
                continue

            @pl.when(half != xh)
            def _(cp=cp):
                cp.start()

            @pl.when(half == xh)
            def _(src=src, dst=dst):
                dst[pl.ds(slot, 1)] = src[pl.ds(z, 1)]

    def spread(name, src, dst):
        base = net.take(8)
        for k in range(1, 8):
            to = (blk + k) % 8
            cp = pltpu.make_async_remote_copy(
                src_ref=src.at[to],
                dst_ref=dst.at[blk],
                send_sem=ss.at[base + k],
                recv_sem=rs.at[base + k],
                device_id=blk_dev(to),
                device_id_type=MESH,
            )
            cp.start()
            first[name, k] = cp
        dst[pl.ds(blk, 1)] = src[pl.ds(blk, 1)]

    spread("w", wts, wt)
    loads[2].wait()
    tok = tk[...].astype(F32)
    xn[...] = scaled(tok, gain_a[...].reshape(1, D))
    start_of = []
    total = jnp.int32(0)
    for i in range(6):
        start_of.append(total)
        total = total + lengths[0, i]

    def segment(index):
        seg = jnp.zeros_like(index)
        begin = jnp.zeros_like(index)
        for s in start_of[1:]:
            seg = seg + (index >= s).astype(jnp.int32)
            begin = jnp.where(index >= s, s, begin)
        return seg, begin

    low = blk - 4
    for k in range(1, 5):

        @pl.when(blk < k)
        def _(k=k):
            near[4 - k] = jnp.zeros((128, 512), BF)

    mine = lax.broadcasted_iota(jnp.int32, (128, 1), 0) + blk * 128
    my_seg, my_begin = segment(mine)

    def wait_first(src, dst, base):
        for j in range(4):
            own = (z == 2 * xh + j // 2) & (xh == j % 2)

            @pl.when(jnp.logical_not(own))
            def _(j=j):
                net.make(src.at[0], dst.at[0], net.dev(c=1), base + j).wait_recv()

    def zcol(base, width, at):
        return pl.ds(pl.multiple_of(base + at * width, 128), width)

    xs = (1, 3, 2)

    class Color:
        def __init__(self, ref, base, width, axes):
            self.ref, self.base, self.width, self.axes = ref, base, width, axes
            self.stage, self.chip = 0, []

        def view(self, axes, **moved):
            at = {"y": y, "x": net.x, "z": z, **moved}
            yy = slice(None) if "y" in axes else at["y"]
            xx = slice(None) if "x" in axes else at["x"] % 2
            hh = slice(None) if "x" in axes else at["x"] // 2
            whole = pl.ds(self.base, 4 * self.width)
            cc = whole if "z" in axes else zcol(self.base, self.width, at["z"])
            return self.ref.at[yy, xx, c, hh, :, cc]

        def go(self):
            axis, done = self.axes[self.stage], self.axes[: self.stage]
            part = self.view(done)
            self.cps = [send(part, net.dev(**{axis: k})) for k in xs]
            self.stage += 1
            if self.stage == 3:
                self.chip.append(send(part, net.dev(c=1)))

        def arrive(self):
            for cp in self.cps:
                cp.wait_recv()

        def land(self, n):
            axis = self.axes[2]
            self.cps[n].wait_recv()
            here = {"y": y, "x": net.x, "z": z}[axis]
            got = self.view(self.axes[:2], **{axis: (here + 4 - xs[n]) % 4})
            self.chip.append(send(got, net.dev(c=1)))

        def close(self):
            for cp in self.chip:
                cp.wait_recv()

    qc = [Color(wq, 512, 256, "xyz"), Color(wq, 0, 128, "xzy"), Color(wq, 1536, 128, "yzx")]
    mc = [Color(wm, 512, 256, "yzx"), Color(wm, 0, 128, "xyz")]
    wait_first(qs, q1, 0)
    block = stack([q1[j] for j in range(4)])
    wq[y, xl, c, xh, :, zcol(0, 128, z)] = block[:, 0:128]
    wq[y, xl, c, xh, :, zcol(512, 256, z)] = block[:, 128:384]
    wq[y, xl, c, xh, :, zcol(1536, 128, z)] = block[:, 384:512]
    for q in qc:
        q.go()
    wait_first(ms, m1, 4)
    block = stack([m1[j] for j in range(4)])
    wm[y, xl, c, xh, :, zcol(0, 128, z)] = block[:, 0:128]
    wm[y, xl, c, xh, :, zcol(512, 256, z)] = block[:, 128:384]
    for m in mc:
        m.go()
    loads[3].wait()
    loads[4].wait()

    for d in range(8):
        es[d] = stack([fe[:, 2 * d], fe[:, 2 * d + 1]])
        os[d] = stack(
            [fo[:, 2 * d + i // 2, i % 2 * 768 : i % 2 * 768 + 768] for i in range(4)]
        )
    for q in qc:
        q.arrive()
        q.go()
    spread("e", es, e1)
    spread("o", os, o1)
    key_at = lax.broadcasted_iota(jnp.int32, (1, 640), 1) + low * 128
    key_seg, _ = segment(key_at)
    msk[...] = jnp.where((my_seg == key_seg) & (key_at <= mine) & (key_at >= 0), 1.0, 0.0).astype(F32)
    lane = lax.broadcasted_iota(jnp.int32, (1, 128), 1)
    step = (lane % 64).astype(F32)
    frequency = jnp.exp(step * (-2.0 * math.log(10000.0) / 128))
    angle = (mine - my_begin).astype(F32) * frequency
    cosine = jnp.cos(angle)
    sine = jnp.where(lane < 64, -jnp.sin(angle), jnp.sin(angle))
    for q in qc:
        q.arrive()
        q.go()
    for m in mc:
        m.arrive()
        m.go()
    for k in range(1, 8):
        first["w", k].wait_recv()
    upper = (
        lax.broadcasted_iota(jnp.int32, (128, 128), 0)
        <= lax.broadcasted_iota(jnp.int32, (128, 128), 1)
    )
    upper = jnp.where(upper, 1.0, 0.0).astype(BF)
    slots = lax.broadcasted_iota(jnp.int32, (64, 128), 0).astype(F32)

    def tables(s, carry):
        w = wt[s]
        member = jnp.where(w > 0, 1.0, 0.0)
        rank = jnp.dot(member.astype(BF), upper, preferred_element_type=F32) - 1.0
        for e in range(2):
            hit = (member[e : e + 1] > 0) & (rank[e : e + 1] == slots)
            oh[s, e * 64 : e * 64 + 64] = jnp.where(hit, 1.0, 0.0).astype(BF)
            ga[s, e * 64 : e * 64 + 64] = jnp.where(hit, w[e : e + 1], 0.0).astype(BF)
        return carry

    lax.fori_loop(0, 8, tables, 0)
    for k in range(1, 8):
        first["e", k].wait_recv()

    def lay_in(i, carry):
        col = pl.ds(pl.multiple_of(i * 256, 256), 256)
        got = [e1[j, :, col].astype(F32) for j in range(8)]
        for e in range(2):
            part = [g[e * 12 : e * 12 + 12] for g in got]
            wi[e, y, xl, c, :, col] = jnp.concatenate(part, axis=0).astype(BF)
        return carry

    def lay_out(i, carry):
        col = pl.ds(pl.multiple_of(i * 256, 256), 256)
        got = [o1[j, :, col].astype(F32) for j in range(8)]
        for n in range(4):
            part = [g[n * 6 : n * 6 + 6] for g in got]
            to = pl.ds(pl.multiple_of(n % 2 * 768 + i * 256, 256), 256)
            wo[n // 2, y, xl, c, :, to] = jnp.concatenate(part, axis=0).astype(BF)
        return carry

    lax.fori_loop(0, 6, lay_in, 0)
    i1 = [send(wi.at[:, y, xl, c], net.xflip())]
    i2 = {k: [send(wi.at[:, y, xl, c], net.dev(y=k))] for k in (1, 3)}
    for k in range(1, 8):
        first["o", k].wait_recv()
    lax.fori_loop(0, 3, lay_out, 0)
    i1.append(send(wo.at[:, y, xl, c], net.xflip()))
    for k in (1, 3):
        i2[k].append(send(wo.at[:, y, xl, c], net.dev(y=k)))
    for m in mc:
        m.arrive()
        m.go()
    for n in range(3):
        for q in qc:
            q.land(n)
    p5 = [send(w.at[:, y, xl, c], net.dev(c=1)) for w in (wi, wo)]
    for q in qc:
        q.close()

    def project(col):
        w = wq[:, :, :, :, :, col].reshape(D, 256)
        return jnp.dot(xn[...], w, preferred_element_type=F32)

    def turned(head):
        return (head * cosine + pltpu.roll(head, 64, 1) * sine).astype(BF)

    kk = project(pl.ds(1536, 256))
    vv = project(pl.ds(1792, 256))
    near[4, :, 0:128] = turned(kk[:, :128])
    near[4, :, 128:256] = turned(kk[:, 128:])
    near[4, :, 256:512] = vv.astype(BF)
    base = net.take(16)
    close_kv, far_kv = {}, {}
    for k in range(1, 8):
        to = blk_dev((blk + k) % 8)
        far_kv[k] = net.make(near.at[4], kv.at[blk], to, base + k)
        if k < 5:
            close_kv[k] = net.make(near.at[4], near.at[4 - k], to, base + 8 + k)

            @pl.when(blk + k < 8)
            def _(k=k):
                close_kv[k].start()


    def query(n, carry):
        p = project(pl.ds(pl.multiple_of(n * 256, 256), 256))
        qh[pl.ds(2 * n, 1)] = turned(p[:, :128])[None]
        qh[pl.ds(2 * n + 1, 1)] = turned(p[:, 128:])[None]
        return carry

    lax.fori_loop(0, 6, query, 0)
    for cp in i1:
        cp.wait_recv()
    i3 = {k: [send(w.at[:, y, 1 - xl, c], net.dev(y=k)) for w in (wi, wo)] for k in (1, 3)}
    p5 += [send(w.at[:, y, 1 - xl, c], net.dev(c=1)) for w in (wi, wo)]
    up, down = net.dev(y=1), net.dev(y=3)
    lo, hi = (y + 3) % 4, (y + 1) % 4
    for k in range(1, 5):

        @pl.when(blk >= k)
        def _(k=k):
            close_kv[k].wait_recv()


    def attend(h, carry):
        g = h // 6
        k = near[:, :, pl.ds(pl.multiple_of(g * 128, 128), 128)].reshape(640, 128)
        v = near[:, :, pl.ds(pl.multiple_of(256 + g * 128, 128), 128)].reshape(640, 128)
        s = lax.dot_general(qh[h], k, (((1,), (1,)), ((), ())), preferred_element_type=F32)
        s = jnp.where(msk[...] > 0, s * (1.0 / math.sqrt(HD)), -1e30)
        w = jnp.exp(s - jnp.max(s, axis=-1, keepdims=True))
        p = (w / jnp.sum(w, axis=-1, keepdims=True)).astype(BF)
        a = jnp.dot(p, v, preferred_element_type=F32)
        at[:, pl.ds(pl.multiple_of(h * 128, 128), 128)] = a.astype(BF)
        return carry

    lax.fori_loop(0, 12, attend, 0)
    for n in range(3):
        for m in mc:
            m.land(n)
    for m in mc:
        m.close()

    def mix(n, carry):
        col = pl.ds(pl.multiple_of(n * 256, 256), 256)
        w = wm[:, :, :, :, :, col].reshape(D, 256)
        hid[:, col] = tk[:, col].astype(F32) + jnp.dot(
            at[...], w, preferred_element_type=F32
        )
        return carry

    lax.fori_loop(0, 6, mix, 0)
    rows[pl.ds(blk, 1)] = scaled(hid[...], gain_m[...].reshape(1, D))[None]
    across = net.dev(x=2)
    t1 = {k: send(rows.at[blk], net.dev(z=k)) for k in xs}
    tx = send(rows.at[blk], across)

    for k in range(1, 8):
        if k > 4:
            far_kv[k].start()
            continue

        @pl.when(blk + k >= 8)
        def _(k=k):
            far_kv[k].start()

    for k in (1, 3):
        for cp in i2[k] + i3[k]:
            cp.wait_recv()
    r4 = [send(w.at[:, lo, 0, c], up) for w in (wi, wo)]
    r4 += [send(w.at[:, hi, 1, c], down) for w in (wi, wo)]
    p6 = [send(w.at[:, v, :, c], net.dev(c=1)) for w in (wi, wo) for v in (lo, hi)]
    tx.wait_recv()
    blk_x = z * 2 + 1 - xh
    t2 = {k: send(rows.at[blk_x], net.dev(z=k)) for k in (1, 3)}
    t1[2].wait_recv()
    blk_o = ((z + 2) % 4) * 2 + xh
    t3 = send(rows.at[blk_o], across)
    for k in (1, 3):
        t1[k].wait_recv()
    for cp in r4:
        cp.wait_recv()
    p6 += [send(w.at[:, (y + 2) % 4, :, c], net.dev(c=1)) for w in (wi, wo)]
    for cp in p5 + p6:
        cp.wait_recv()

    order = (0, 1, 3, 2)

    def experts(plane, out):
        for j, dz in enumerate(order):
            s = ((z + dz) % 4) * 2 + plane

            def pick(n, carry, s=s, j=j):
                col = pl.ds(pl.multiple_of(n * 512, 512), 512)
                got = jnp.dot(oh[s], rows[s, :, col], preferred_element_type=F32).astype(BF)
                ch[0, j * 64 : j * 64 + 64, col] = got[:64]
                ch[1, j * 64 : j * 64 + 64, col] = got[64:]
                return carry

            lax.fori_loop(0, 3, pick, 0)

        def one(e, carry):
            def gate(n, carry):
                lo_col = pl.ds(pl.multiple_of(n * 256, 256), 256)
                up_col = pl.ds(pl.multiple_of(768 + n * 256, 256), 256)
                a = jnp.dot(
                    ch[e], wi[e, :, :, :, :, lo_col].reshape(D, 256), preferred_element_type=F32
                )
                b = jnp.dot(
                    ch[e], wi[e, :, :, :, :, up_col].reshape(D, 256), preferred_element_type=F32
                )
                act[:, lo_col] = (jnp.maximum(a, 0.0) * b).astype(BF)
                return carry

            lax.fori_loop(0, 3, gate, 0)

            def down_to(n, carry):
                col = pl.ds(pl.multiple_of(n * 256, 256), 256)
                r = jnp.dot(
                    act[...], wo[e, :, :, :, :, col].reshape(FF, 256), preferred_element_type=F32
                ).astype(BF)
                for j in range(4):
                    res[j, pl.ds(pl.multiple_of(e * 64, 64), 64), col] = r[j * 64 : j * 64 + 64]
                return carry

            lax.fori_loop(0, 6, down_to, 0)
            return carry

        lax.fori_loop(0, 2, one, 0)
        for j, dz in enumerate(order):
            s = ((z + dz) % 4) * 2 + plane

            def fold(n, carry, s=s, j=j, dz=dz):
                col = pl.ds(pl.multiple_of(n * 512, 512), 512)
                t = lax.dot_general(
                    ga[s], res[j, :, col], (((0,), (0,)), ((), ())), preferred_element_type=F32
                )
                if out is pa and dz == 0:
                    hid[:, col] = hid[:, col] + t
                else:
                    out[dz, :, col] = t.astype(BF)
                return carry

            lax.fori_loop(0, 3, fold, 0)

    experts(xh, pa)
    s1 = [send(pa.at[k], net.dev(z=k), ra.at[k // 2]) for k in (1, 3)]
    for cp in t2.values():
        cp.wait_recv()
    t3.wait_recv()
    experts(1 - xh, pb)
    s2 = [send(pb.at[2], across, rx.at[0])]
    s3 = [send(pb.at[k], net.dev(z=k), rb.at[k // 2]) for k in (1, 3)]
    for cp in s1:
        cp.wait_recv()
    hid[...] = hid[...] + ra[0].astype(F32) + ra[1].astype(F32)
    s2[0].wait_recv()
    pa[2] = (pa[2].astype(F32) + rx[0].astype(F32)).astype(BF)
    s4 = send(pa.at[2], net.dev(z=2), rz)
    for cp in s3:
        cp.wait_recv()
    pb[0] = (pb[0].astype(F32) + rb[0].astype(F32) + rb[1].astype(F32)).astype(BF)
    s5 = send(pb.at[0], across, rx.at[1])
    kv[pl.ds(blk, 1)] = near[4][None]
    for k in range(1, 8):
        if k > 4:
            far_kv[k].wait_recv()
            far_kv[k].wait_send()
            continue

        @pl.when(blk < k)
        def _(k=k):
            far_kv[k].wait_recv()

        @pl.when(blk >= k)
        def _(k=k):
            kv[pl.ds(blk - k, 1)] = near[4 - k][None]

        @pl.when(blk + k < 8)
        def _(k=k):
            close_kv[k].wait_send()

        @pl.when(blk + k >= 8)
        def _(k=k):
            far_kv[k].wait_send()

    logical = jnp.int32(0)
    for i in range(8):
        logical = jnp.where(table[0, i] == blk, i, logical)
    pages[...] = kv[logical]
    s4.wait_recv()
    s5.wait_recv()
    mixed[...] = (hid[...] + rz[...].astype(F32) + rx[1].astype(F32)).astype(BF)
    for (name, k), cp in first.items():
        if k:
            cp.wait_send()
        else:

            @pl.when(half != xh)
            def _(cp=cp):
                cp.wait_send()

    for cp in sent:
        cp.wait_send()


def layer_call(*args):
    vm = pl.BlockSpec(memory_space=pltpu.VMEM)
    sm = pl.BlockSpec(memory_space=pltpu.SMEM)
    return pl.pallas_call(
        layer_kernel,
        out_shape=(
            jax.ShapeDtypeStruct((128, D), BF),
            jax.ShapeDtypeStruct((128, 512), BF),
        ),
        in_specs=[pl.BlockSpec(memory_space=pl.ANY)] * 5 + [vm] * 3 + [sm] * 2,
        out_specs=(vm,) * 2,
        scratch_shapes=[
            pltpu.VMEM((4, 2, 2, 2, 48, 2048), BF),
            pltpu.VMEM((4, 2, 2, 2, 48, D), BF),
            pltpu.VMEM((2, 4, 2, 2, 96, D), BF),
            pltpu.VMEM((2, 4, 2, 2, 48, D), BF),
            pltpu.VMEM((12, 2048), F32),
            pltpu.VMEM((12, D), F32),
            pltpu.VMEM((12, 16, D), F32),
            pltpu.VMEM((6, 16, D), F32),
            pltpu.VMEM((128, D), BF),
            pltpu.VMEM((4, 12, 512), BF),
            pltpu.VMEM((4, 12, 384), BF),
            pltpu.VMEM((8, 24, D), BF),
            pltpu.VMEM((8, 24, FF), BF),
            pltpu.VMEM((4, 12, 512), BF),
            pltpu.VMEM((4, 12, 384), BF),
            pltpu.VMEM((8, 24, D), BF),
            pltpu.VMEM((8, 24, FF), BF),
            pltpu.VMEM((8, 2, 128), F32),
            pltpu.VMEM((128, D), BF),
            pltpu.VMEM((12, 128, 128), BF),
            pltpu.VMEM((8, 128, 512), BF),
            pltpu.VMEM((5, 128, 512), BF),
            pltpu.VMEM((128, D), BF),
            pltpu.VMEM((128, D), F32),
            pltpu.VMEM((8, 128, D), BF),
            pltpu.VMEM((8, 128, 128), BF),
            pltpu.VMEM((8, 128, 128), BF),
            pltpu.VMEM((128, 640), F32),
            pltpu.VMEM((2, 256, D), BF),
            pltpu.VMEM((256, FF), BF),
            pltpu.VMEM((4, 128, D), BF),
            pltpu.VMEM((4, 128, D), BF),
            pltpu.VMEM((4, 128, D), BF),
            pltpu.VMEM((2, 128, D), BF),
            pltpu.VMEM((2, 128, D), BF),
            pltpu.VMEM((2, 128, D), BF),
            pltpu.VMEM((128, D), BF),
            pltpu.SemaphoreType.DMA((5,)),
            pltpu.SemaphoreType.DMA((200,)),
            pltpu.SemaphoreType.DMA((200,)),
        ],
        compiler_params=pltpu.CompilerParams(
            collective_id=0, has_side_effects=True, vmem_limit_bytes=64 << 20
        ),
    )(*args)


def body(
    tokens,
    attn_in,
    attn_out,
    expert_in,
    expert_out,
    attn_gain,
    moe_gain,
    lengths,
    page_table,
    routes,
    gates,
):
    ids = jnp.arange(E, dtype=jnp.int32)
    weight = jnp.sum(
        jnp.where(
            routes.T[None, :, :] == ids[:, None, None], gates.astype(F32).T[None, :, :], 0.0
        ),
        axis=1,
    ).reshape(8, 2, 128)
    mixed, pages = layer_call(
        attn_in,
        attn_out,
        expert_in.transpose(1, 0, 2),
        expert_out.transpose(1, 0, 2),
        tokens,
        weight,
        attn_gain,
        moe_gain,
        lengths,
        page_table,
    )
    return mixed, pages[None]


def solution(mesh):
    in_specs = (
        P(("rep", "blk"), None),
        P(("rep", "blk"), None),
        P(("rep", "blk"), None),
        P(None, ("rep", "blk"), None),
        P(None, ("rep", "blk"), None),
        P(),
        P(),
        P("rep", None),
        P("rep", None),
        P(("rep", "blk"), None),
        P(("rep", "blk"), None),
    )
    out_specs = (P(("rep", "blk"), None), P(("rep", "blk"), None, None))
    return jax.shard_map(body, mesh=mesh, in_specs=in_specs, out_specs=out_specs, check_vma=False)
```

```python
import math

import jax
import jax.numpy as jnp
from jax import lax
from jax.experimental import pallas as pl
from jax.experimental.pallas import tpu as pltpu
from jax.sharding import PartitionSpec as P

D = 1536
FF = 768
QH = 12
KVH = 2
HD = 128
E = 16
PAGE = 128
CAP = 64
QW = 1536
BF = jnp.bfloat16
F32 = jnp.float32
MESH = pl.DeviceIdType.MESH


class Net:
    def __init__(self, send_sems, recv_sems):
        rep, blk = lax.axis_index("rep"), lax.axis_index("blk")
        self.y, self.xl, self.c = rep // 4, (rep // 2) % 2, rep % 2
        self.z, self.xh = blk // 2, blk % 2
        self.x = self.xh * 2 + self.xl
        self.ss, self.rs, self.used = send_sems, recv_sems, 0

    def dev(self, y=0, x=0, z=0, c=0):
        yy = (self.y + y) % 4
        xx = (self.x + x) % 4
        zz = (self.z + z) % 4
        cc = (self.c + c) % 2
        return ((yy * 2 + xx % 2) * 2 + cc, zz * 2 + xx // 2)

    def xflip(self):
        return (((self.y * 2 + 1 - self.xl) * 2) + self.c, self.z * 2 + self.xh)

    def take(self, n=1):
        k = self.used
        self.used = k + n
        return k

    def make(self, src, dst, to, k):
        return pltpu.make_async_remote_copy(
            src_ref=src,
            dst_ref=dst,
            send_sem=self.ss.at[k],
            recv_sem=self.rs.at[k],
            device_id=to,
            device_id_type=MESH,
        )

    def send(self, ref, to):
        cp = self.make(ref, ref, to, self.take())
        cp.start()
        return cp


def enter(net):
    barrier = pltpu.get_barrier_semaphore()
    around = [net.dev(x=1), net.dev(x=3), net.dev(c=1)]
    around += [net.dev(y=k) for k in (1, 2, 3)]
    around += [net.dev(z=dz, x=dx) for dz in range(4) for dx in (0, 2) if dz or dx]
    for to in around:
        pl.semaphore_signal(barrier, inc=1, device_id=to, device_id_type=MESH)
    pl.semaphore_wait(barrier, len(around))


def scaled(values, gain):
    mean_sq = jnp.mean(values * values, axis=-1, keepdims=True)
    return (values * lax.rsqrt(mean_sq + 1e-06) * gain).astype(BF)


def stack(pieces):
    return jnp.concatenate([p.astype(F32) for p in pieces], axis=0).astype(BF)


def layer_kernel(
    xq,
    xm,
    xe,
    xo,
    tokens,
    wts,
    gain_a,
    gain_m,
    lengths,
    table,
    mixed,
    pages,
    wq,
    wm,
    wi,
    wo,
    fq,
    fm,
    fe,
    fo,
    tk,
    qs,
    ms,
    es,
    os,
    q1,
    m1,
    e1,
    o1,
    wt,
    xn,
    qh,
    kv,
    near,
    at,
    hid,
    rows,
    oh,
    ga,
    msk,
    ch,
    act,
    res,
    pa,
    pb,
    ra,
    rb,
    rx,
    rz,
    ls,
    ss,
    rs,
):
    net = Net(ss, rs)
    y, xl, c, z, xh = net.y, net.xl, net.c, net.z, net.xh
    blk = z * 2 + xh
    sent = []

    def send(ref, to, dst=None):
        cp = net.make(ref, ref if dst is None else dst, to, net.take())
        cp.start()
        sent.append(cp)
        return cp

    def blk_dev(b):
        return ((y * 2 + xl) * 2 + c, b)

    loads = []
    for n, (src, dst) in enumerate(
        ((xq, fq), (xm, fm), (tokens, tk), (xe, fe), (xo, fo))
    ):
        cp = pltpu.make_async_copy(src, dst, ls.at[n])
        cp.start()
        loads.append(cp)
    loads[0].wait()
    for k in range(4):
        qs[k, :, 0:128] = fq[:, k * 128 : k * 128 + 128].astype(BF)
        qs[k, :, 128:384] = fq[:, 512 + k * 256 : 768 + k * 256].astype(BF)
        qs[k, :, 384:512] = fq[:, 1536 + k * 128 : 1664 + k * 128].astype(BF)
    loads[1].wait()
    for k in range(4):
        ms[k, :, 0:128] = fm[:, k * 128 : k * 128 + 128].astype(BF)
        ms[k, :, 128:384] = fm[:, 512 + k * 256 : 768 + k * 256].astype(BF)
    enter(net)
    half = z // 2
    slot = (z % 2) * 2 + xh
    first = {}
    for name, src, dst in (("q", qs, q1), ("m", ms, m1)):
        base = net.take(4)
        for k in range(4):
            zt = (z + k) % 4
            cp = pltpu.make_async_remote_copy(
                src_ref=src.at[zt],
                dst_ref=dst.at[slot],
                send_sem=ss.at[base + k],
                recv_sem=rs.at[base + slot],
                device_id=((y * 2 + xl) * 2 + c, zt * 2 + half),
                device_id_type=MESH,
            )
            first[name, k] = cp
            if k:
                cp.start()
                continue

            @pl.when(half != xh)
            def _(cp=cp):
                cp.start()

            @pl.when(half == xh)
            def _(src=src, dst=dst):
                dst[pl.ds(slot, 1)] = src[pl.ds(z, 1)]

    def spread(name, src, dst):
        base = net.take(8)
        for k in range(1, 8):
            to = (blk + k) % 8
            cp = pltpu.make_async_remote_copy(
                src_ref=src.at[to],
                dst_ref=dst.at[blk],
                send_sem=ss.at[base + k],
                recv_sem=rs.at[base + k],
                device_id=blk_dev(to),
                device_id_type=MESH,
            )
            cp.start()
            first[name, k] = cp
        dst[pl.ds(blk, 1)] = src[pl.ds(blk, 1)]

    spread("w", wts, wt)
    loads[2].wait()
    tok = tk[...].astype(F32)
    xn[...] = scaled(tok, gain_a[...].reshape(1, D))
    start_of = []
    total = jnp.int32(0)
    for i in range(6):
        start_of.append(total)
        total = total + lengths[0, i]

    def segment(index):
        seg = jnp.zeros_like(index)
        begin = jnp.zeros_like(index)
        for s in start_of[1:]:
            seg = seg + (index >= s).astype(jnp.int32)
            begin = jnp.where(index >= s, s, begin)
        return seg, begin

    low = blk - 4
    for k in range(1, 5):

        @pl.when(blk < k)
        def _(k=k):
            near[4 - k] = jnp.zeros((128, 512), BF)

    mine = lax.broadcasted_iota(jnp.int32, (128, 1), 0) + blk * 128
    my_seg, my_begin = segment(mine)

    def wait_first(src, dst, base):
        for j in range(4):
            own = (z == 2 * xh + j // 2) & (xh == j % 2)

            @pl.when(jnp.logical_not(own))
            def _(j=j):
                net.make(src.at[0], dst.at[0], net.dev(c=1), base + j).wait_recv()

    def zcol(base, width, at):
        return pl.ds(pl.multiple_of(base + at * width, 128), width)

    xs = (1, 3, 2)

    class Color:
        def __init__(self, ref, base, width, axes):
            self.ref, self.base, self.width, self.axes = ref, base, width, axes
            self.stage, self.chip = 0, []

        def view(self, axes, **moved):
            at = {"y": y, "x": net.x, "z": z, **moved}
            yy = slice(None) if "y" in axes else at["y"]
            xx = slice(None) if "x" in axes else at["x"] % 2
            hh = slice(None) if "x" in axes else at["x"] // 2
            whole = pl.ds(self.base, 4 * self.width)
            cc = whole if "z" in axes else zcol(self.base, self.width, at["z"])
            return self.ref.at[yy, xx, c, hh, :, cc]

        def go(self):
            axis, done = self.axes[self.stage], self.axes[: self.stage]
            part = self.view(done)
            self.cps = [send(part, net.dev(**{axis: k})) for k in xs]
            self.stage += 1
            if self.stage == 3:
                self.chip.append(send(part, net.dev(c=1)))

        def arrive(self):
            for cp in self.cps:
                cp.wait_recv()

        def land(self, n):
            axis = self.axes[2]
            self.cps[n].wait_recv()
            here = {"y": y, "x": net.x, "z": z}[axis]
            got = self.view(self.axes[:2], **{axis: (here + 4 - xs[n]) % 4})
            self.chip.append(send(got, net.dev(c=1)))

        def close(self):
            for cp in self.chip:
                cp.wait_recv()

    qc = [Color(wq, 512, 256, "xyz"), Color(wq, 0, 128, "xzy"), Color(wq, 1536, 128, "yzx")]
    mc = [Color(wm, 512, 256, "yzx"), Color(wm, 0, 128, "xyz")]
    wait_first(qs, q1, 0)
    block = stack([q1[j] for j in range(4)])
    wq[y, xl, c, xh, :, zcol(0, 128, z)] = block[:, 0:128]
    wq[y, xl, c, xh, :, zcol(512, 256, z)] = block[:, 128:384]
    wq[y, xl, c, xh, :, zcol(1536, 128, z)] = block[:, 384:512]
    for q in qc:
        q.go()
    wait_first(ms, m1, 4)
    block = stack([m1[j] for j in range(4)])
    wm[y, xl, c, xh, :, zcol(0, 128, z)] = block[:, 0:128]
    wm[y, xl, c, xh, :, zcol(512, 256, z)] = block[:, 128:384]
    for m in mc:
        m.go()
    loads[3].wait()
    loads[4].wait()

    for d in range(8):
        es[d] = stack([fe[:, 2 * d], fe[:, 2 * d + 1]])
        os[d] = stack(
            [fo[:, 2 * d + i // 2, i % 2 * 768 : i % 2 * 768 + 768] for i in range(4)]
        )
    for q in qc:
        q.arrive()
        q.go()
    spread("e", es, e1)
    spread("o", os, o1)
    key_at = lax.broadcasted_iota(jnp.int32, (1, 640), 1) + low * 128
    key_seg, _ = segment(key_at)
    msk[...] = jnp.where((my_seg == key_seg) & (key_at <= mine) & (key_at >= 0), 1.0, 0.0).astype(F32)
    lane = lax.broadcasted_iota(jnp.int32, (1, 128), 1)
    step = (lane % 64).astype(F32)
    frequency = jnp.exp(step * (-2.0 * math.log(10000.0) / 128))
    angle = (mine - my_begin).astype(F32) * frequency
    cosine = jnp.cos(angle)
    sine = jnp.where(lane < 64, -jnp.sin(angle), jnp.sin(angle))
    for q in qc:
        q.arrive()
        q.go()
    for m in mc:
        m.arrive()
        m.go()
    for k in range(1, 8):
        first["w", k].wait_recv()
    upper = (
        lax.broadcasted_iota(jnp.int32, (128, 128), 0)
        <= lax.broadcasted_iota(jnp.int32, (128, 128), 1)
    )
    upper = jnp.where(upper, 1.0, 0.0).astype(BF)
    slots = lax.broadcasted_iota(jnp.int32, (64, 128), 0).astype(F32)

    def tables(s, carry):
        w = wt[s]
        member = jnp.where(w > 0, 1.0, 0.0)
        rank = jnp.dot(member.astype(BF), upper, preferred_element_type=F32) - 1.0
        for e in range(2):
            hit = (member[e : e + 1] > 0) & (rank[e : e + 1] == slots)
            oh[s, e * 64 : e * 64 + 64] = jnp.where(hit, 1.0, 0.0).astype(BF)
            ga[s, e * 64 : e * 64 + 64] = jnp.where(hit, w[e : e + 1], 0.0).astype(BF)
        return carry

    lax.fori_loop(0, 8, tables, 0)
    for k in range(1, 8):
        first["e", k].wait_recv()

    def lay_in(i, carry):
        col = pl.ds(pl.multiple_of(i * 256, 256), 256)
        got = [e1[j, :, col].astype(F32) for j in range(8)]
        for e in range(2):
            part = [g[e * 12 : e * 12 + 12] for g in got]
            wi[e, y, xl, c, :, col] = jnp.concatenate(part, axis=0).astype(BF)
        return carry

    def lay_out(i, carry):
        col = pl.ds(pl.multiple_of(i * 256, 256), 256)
        got = [o1[j, :, col].astype(F32) for j in range(8)]
        for n in range(4):
            part = [g[n * 6 : n * 6 + 6] for g in got]
            to = pl.ds(pl.multiple_of(n % 2 * 768 + i * 256, 256), 256)
            wo[n // 2, y, xl, c, :, to] = jnp.concatenate(part, axis=0).astype(BF)
        return carry

    lax.fori_loop(0, 6, lay_in, 0)
    i1 = [send(wi.at[:, y, xl, c], net.xflip())]
    i2 = {k: [send(wi.at[:, y, xl, c], net.dev(y=k))] for k in (1, 3)}
    for k in range(1, 8):
        first["o", k].wait_recv()
    lax.fori_loop(0, 3, lay_out, 0)
    i1.append(send(wo.at[:, y, xl, c], net.xflip()))
    for k in (1, 3):
        i2[k].append(send(wo.at[:, y, xl, c], net.dev(y=k)))
    for m in mc:
        m.arrive()
        m.go()
    for n in range(3):
        for q in qc:
            q.land(n)
    p5 = [send(w.at[:, y, xl, c], net.dev(c=1)) for w in (wi, wo)]
    for q in qc:
        q.close()

    def project(col):
        w = wq[:, :, :, :, :, col].reshape(D, 256)
        return jnp.dot(xn[...], w, preferred_element_type=F32)

    def turned(head):
        return (head * cosine + pltpu.roll(head, 64, 1) * sine).astype(BF)

    kk = project(pl.ds(1536, 256))
    vv = project(pl.ds(1792, 256))
    near[4, :, 0:128] = turned(kk[:, :128])
    near[4, :, 128:256] = turned(kk[:, 128:])
    near[4, :, 256:512] = vv.astype(BF)
    base = net.take(16)
    close_kv, far_kv = {}, {}
    for k in range(1, 8):
        to = blk_dev((blk + k) % 8)
        far_kv[k] = net.make(near.at[4], kv.at[blk], to, base + k)
        if k < 5:
            close_kv[k] = net.make(near.at[4], near.at[4 - k], to, base + 8 + k)

            @pl.when(blk + k < 8)
            def _(k=k):
                close_kv[k].start()


    def query(n, carry):
        p = project(pl.ds(pl.multiple_of(n * 256, 256), 256))
        qh[pl.ds(2 * n, 1)] = turned(p[:, :128])[None]
        qh[pl.ds(2 * n + 1, 1)] = turned(p[:, 128:])[None]
        return carry

    lax.fori_loop(0, 6, query, 0)
    for cp in i1:
        cp.wait_recv()
    i3 = {k: [send(w.at[:, y, 1 - xl, c], net.dev(y=k)) for w in (wi, wo)] for k in (1, 3)}
    p5 += [send(w.at[:, y, 1 - xl, c], net.dev(c=1)) for w in (wi, wo)]
    up, down = net.dev(y=1), net.dev(y=3)
    lo, hi = (y + 3) % 4, (y + 1) % 4
    for k in range(1, 5):

        @pl.when(blk >= k)
        def _(k=k):
            close_kv[k].wait_recv()


    for k in range(1, 8):
        if k > 4:
            far_kv[k].start()
            continue

        @pl.when(blk + k >= 8)
        def _(k=k):
            far_kv[k].start()

    def attend(h, carry):
        g = h // 6
        k = near[:, :, pl.ds(pl.multiple_of(g * 128, 128), 128)].reshape(640, 128)
        v = near[:, :, pl.ds(pl.multiple_of(256 + g * 128, 128), 128)].reshape(640, 128)
        s = lax.dot_general(qh[h], k, (((1,), (1,)), ((), ())), preferred_element_type=F32)
        s = jnp.where(msk[...] > 0, s * (1.0 / math.sqrt(HD)), -1e30)
        w = jnp.exp(s - jnp.max(s, axis=-1, keepdims=True))
        p = (w / jnp.sum(w, axis=-1, keepdims=True)).astype(BF)
        a = jnp.dot(p, v, preferred_element_type=F32)
        at[:, pl.ds(pl.multiple_of(h * 128, 128), 128)] = a.astype(BF)
        return carry

    lax.fori_loop(0, 12, attend, 0)
    for n in range(3):
        for m in mc:
            m.land(n)
    for m in mc:
        m.close()

    def mix(n, carry):
        col = pl.ds(pl.multiple_of(n * 256, 256), 256)
        w = wm[:, :, :, :, :, col].reshape(D, 256)
        hid[:, col] = tk[:, col].astype(F32) + jnp.dot(
            at[...], w, preferred_element_type=F32
        )
        return carry

    lax.fori_loop(0, 6, mix, 0)
    rows[pl.ds(blk, 1)] = scaled(hid[...], gain_m[...].reshape(1, D))[None]
    across = net.dev(x=2)
    t1 = {k: send(rows.at[blk], net.dev(z=k)) for k in xs}
    tx = send(rows.at[blk], across)

    for k in (1, 3):
        for cp in i2[k] + i3[k]:
            cp.wait_recv()
    r4 = [send(w.at[:, lo, 0, c], up) for w in (wi, wo)]
    r4 += [send(w.at[:, hi, 1, c], down) for w in (wi, wo)]
    p6 = [send(w.at[:, v, :, c], net.dev(c=1)) for w in (wi, wo) for v in (lo, hi)]
    tx.wait_recv()
    blk_x = z * 2 + 1 - xh
    t2 = {k: send(rows.at[blk_x], net.dev(z=k)) for k in (1, 3)}
    t1[2].wait_recv()
    blk_o = ((z + 2) % 4) * 2 + xh
    t3 = send(rows.at[blk_o], across)
    for k in (1, 3):
        t1[k].wait_recv()
    for cp in r4:
        cp.wait_recv()
    p6 += [send(w.at[:, (y + 2) % 4, :, c], net.dev(c=1)) for w in (wi, wo)]
    for cp in p5 + p6:
        cp.wait_recv()

    order = (0, 1, 3, 2)

    def experts(plane, out):
        for j, dz in enumerate(order):
            s = ((z + dz) % 4) * 2 + plane

            def pick(n, carry, s=s, j=j):
                col = pl.ds(pl.multiple_of(n * 512, 512), 512)
                got = jnp.dot(oh[s], rows[s, :, col], preferred_element_type=F32).astype(BF)
                ch[0, j * 64 : j * 64 + 64, col] = got[:64]
                ch[1, j * 64 : j * 64 + 64, col] = got[64:]
                return carry

            lax.fori_loop(0, 3, pick, 0)

        def one(e, carry):
            def gate(n, carry):
                lo_col = pl.ds(pl.multiple_of(n * 256, 256), 256)
                up_col = pl.ds(pl.multiple_of(768 + n * 256, 256), 256)
                a = jnp.dot(
                    ch[e], wi[e, :, :, :, :, lo_col].reshape(D, 256), preferred_element_type=F32
                )
                b = jnp.dot(
                    ch[e], wi[e, :, :, :, :, up_col].reshape(D, 256), preferred_element_type=F32
                )
                act[:, lo_col] = (jnp.maximum(a, 0.0) * b).astype(BF)
                return carry

            lax.fori_loop(0, 3, gate, 0)

            def down_to(n, carry):
                col = pl.ds(pl.multiple_of(n * 256, 256), 256)
                r = jnp.dot(
                    act[...], wo[e, :, :, :, :, col].reshape(FF, 256), preferred_element_type=F32
                ).astype(BF)
                for j in range(4):
                    res[j, pl.ds(pl.multiple_of(e * 64, 64), 64), col] = r[j * 64 : j * 64 + 64]
                return carry

            lax.fori_loop(0, 6, down_to, 0)
            return carry

        lax.fori_loop(0, 2, one, 0)
        for j, dz in enumerate(order):
            s = ((z + dz) % 4) * 2 + plane

            def fold(n, carry, s=s, j=j, dz=dz):
                col = pl.ds(pl.multiple_of(n * 512, 512), 512)
                t = lax.dot_general(
                    ga[s], res[j, :, col], (((0,), (0,)), ((), ())), preferred_element_type=F32
                )
                if out is pa and dz == 0:
                    hid[:, col] = hid[:, col] + t
                else:
                    out[dz, :, col] = t.astype(BF)
                return carry

            lax.fori_loop(0, 3, fold, 0)

    experts(xh, pa)
    s1 = [send(pa.at[k], net.dev(z=k), ra.at[k // 2]) for k in (1, 3)]
    for cp in t2.values():
        cp.wait_recv()
    t3.wait_recv()
    experts(1 - xh, pb)
    s2 = [send(pb.at[2], across, rx.at[0])]
    s3 = [send(pb.at[k], net.dev(z=k), rb.at[k // 2]) for k in (1, 3)]
    for cp in s1:
        cp.wait_recv()
    hid[...] = hid[...] + ra[0].astype(F32) + ra[1].astype(F32)
    s2[0].wait_recv()
    pa[2] = (pa[2].astype(F32) + rx[0].astype(F32)).astype(BF)
    s4 = send(pa.at[2], net.dev(z=2), rz)
    for cp in s3:
        cp.wait_recv()
    pb[0] = (pb[0].astype(F32) + rb[0].astype(F32) + rb[1].astype(F32)).astype(BF)
    s5 = send(pb.at[0], across, rx.at[1])
    kv[pl.ds(blk, 1)] = near[4][None]
    for k in range(1, 8):
        if k > 4:
            far_kv[k].wait_recv()
            far_kv[k].wait_send()
            continue

        @pl.when(blk < k)
        def _(k=k):
            far_kv[k].wait_recv()

        @pl.when(blk >= k)
        def _(k=k):
            kv[pl.ds(blk - k, 1)] = near[4 - k][None]

        @pl.when(blk + k < 8)
        def _(k=k):
            close_kv[k].wait_send()

        @pl.when(blk + k >= 8)
        def _(k=k):
            far_kv[k].wait_send()

    logical = jnp.int32(0)
    for i in range(8):
        logical = jnp.where(table[0, i] == blk, i, logical)
    pages[...] = kv[logical]
    s4.wait_recv()
    s5.wait_recv()
    mixed[...] = (hid[...] + rz[...].astype(F32) + rx[1].astype(F32)).astype(BF)
    for (name, k), cp in first.items():
        if k:
            cp.wait_send()
        else:

            @pl.when(half != xh)
            def _(cp=cp):
                cp.wait_send()

    for cp in sent:
        cp.wait_send()


def layer_call(*args):
    vm = pl.BlockSpec(memory_space=pltpu.VMEM)
    sm = pl.BlockSpec(memory_space=pltpu.SMEM)
    return pl.pallas_call(
        layer_kernel,
        out_shape=(
            jax.ShapeDtypeStruct((128, D), BF),
            jax.ShapeDtypeStruct((128, 512), BF),
        ),
        in_specs=[pl.BlockSpec(memory_space=pl.ANY)] * 5 + [vm] * 3 + [sm] * 2,
        out_specs=(vm,) * 2,
        scratch_shapes=[
            pltpu.VMEM((4, 2, 2, 2, 48, 2048), BF),
            pltpu.VMEM((4, 2, 2, 2, 48, D), BF),
            pltpu.VMEM((2, 4, 2, 2, 96, D), BF),
            pltpu.VMEM((2, 4, 2, 2, 48, D), BF),
            pltpu.VMEM((12, 2048), F32),
            pltpu.VMEM((12, D), F32),
            pltpu.VMEM((12, 16, D), F32),
            pltpu.VMEM((6, 16, D), F32),
            pltpu.VMEM((128, D), BF),
            pltpu.VMEM((4, 12, 512), BF),
            pltpu.VMEM((4, 12, 384), BF),
            pltpu.VMEM((8, 24, D), BF),
            pltpu.VMEM((8, 24, FF), BF),
            pltpu.VMEM((4, 12, 512), BF),
            pltpu.VMEM((4, 12, 384), BF),
            pltpu.VMEM((8, 24, D), BF),
            pltpu.VMEM((8, 24, FF), BF),
            pltpu.VMEM((8, 2, 128), F32),
            pltpu.VMEM((128, D), BF),
            pltpu.VMEM((12, 128, 128), BF),
            pltpu.VMEM((8, 128, 512), BF),
            pltpu.VMEM((5, 128, 512), BF),
            pltpu.VMEM((128, D), BF),
            pltpu.VMEM((128, D), F32),
            pltpu.VMEM((8, 128, D), BF),
            pltpu.VMEM((8, 128, 128), BF),
            pltpu.VMEM((8, 128, 128), BF),
            pltpu.VMEM((128, 640), F32),
            pltpu.VMEM((2, 256, D), BF),
            pltpu.VMEM((256, FF), BF),
            pltpu.VMEM((4, 128, D), BF),
            pltpu.VMEM((4, 128, D), BF),
            pltpu.VMEM((4, 128, D), BF),
            pltpu.VMEM((2, 128, D), BF),
            pltpu.VMEM((2, 128, D), BF),
            pltpu.VMEM((2, 128, D), BF),
            pltpu.VMEM((128, D), BF),
            pltpu.SemaphoreType.DMA((5,)),
            pltpu.SemaphoreType.DMA((200,)),
            pltpu.SemaphoreType.DMA((200,)),
        ],
        compiler_params=pltpu.CompilerParams(
            collective_id=0, has_side_effects=True, vmem_limit_bytes=64 << 20
        ),
    )(*args)


def body(
    tokens,
    attn_in,
    attn_out,
    expert_in,
    expert_out,
    attn_gain,
    moe_gain,
    lengths,
    page_table,
    routes,
    gates,
):
    ids = jnp.arange(E, dtype=jnp.int32)
    weight = jnp.sum(
        jnp.where(
            routes.T[None, :, :] == ids[:, None, None], gates.astype(F32).T[None, :, :], 0.0
        ),
        axis=1,
    ).reshape(8, 2, 128)
    mixed, pages = layer_call(
        attn_in,
        attn_out,
        expert_in.transpose(1, 0, 2),
        expert_out.transpose(1, 0, 2),
        tokens,
        weight,
        attn_gain,
        moe_gain,
        lengths,
        page_table,
    )
    return mixed, pages[None]


def solution(mesh):
    in_specs = (
        P(("rep", "blk"), None),
        P(("rep", "blk"), None),
        P(("rep", "blk"), None),
        P(None, ("rep", "blk"), None),
        P(None, ("rep", "blk"), None),
        P(),
        P(),
        P("rep", None),
        P("rep", None),
        P(("rep", "blk"), None),
        P(("rep", "blk"), None),
    )
    out_specs = (P(("rep", "blk"), None), P(("rep", "blk"), None, None))
    return jax.shard_map(body, mesh=mesh, in_specs=in_specs, out_specs=out_specs, check_vma=False)
```
